512 devices in a mesh: walk: 64 (over z, y), col: 8 (over x, core).
Axes of the slice: x: 4, y: 4, z: 16, core: 2. Of those that a mesh axis runs over, the one named last changes fastest.
Arguments:
- jacobian: float32 [384, 524288], P('walk', 'col'), may hold values from -25 to 25
- prev_update: float32 [8, 65536], P('col', 'walk'), may hold values from -6 to 6
- base_energy: float32 [384], P('walk'), may hold values from -6 to 6
- elec_pos: float32 [384, 3, 66], P('walk'), may hold values from -8 to 8
- atom_pos: float32 [3, 21], replicated, may hold values from -6 to 6
- quad_ratio: float32 [384, 21, 66, 12], P('walk'), may hold values from -1.2 to 1.2
- rotation: int32 [384, 66], P('walk'), may hold values from 0 to 15
- channels: int32 [21], replicated, may hold values from 1 to 3
- ecp_coef: float32 [21, 3], replicated, may hold values from 0.5 to 2
- ecp_expo: float32 [21, 3], replicated, may hold values from 0.2 to 2
Outputs:
- local_energy: float32 [384], P('walk')
- update: float32 [8, 65536], P('col', 'walk')
The draws below stay inside these ranges and needn't reach their ends.
All inputs are finite; a program needn't handle non-finite values.
Results may differ from the reference program's by a relative error of at most 0.0003.
Values sent between devices are 32-bit elements; how exact they have to be, the bound alone decides.
No kernel may reach another device: no remote copies, remote signals or barrier semaphores. Data moves between devices by JAX's collectives and lax.ppermute only.
A program may use at most 64 MiB of HBM per device.

```python
import math
import jax
import jax.numpy as jnp
from jax import lax

NE = 66
NA = 21
QUAD = 12
LMAX = 3
NROT = 16
WALKERS = 384
PARAMS = 524288
N_COL = 8


def draw_jacobian(key, part):
    keys = jax.random.split(key, 4)
    noise = jnp.clip(jax.random.normal(keys[0], (WALKERS, PARAMS), jnp.float32), -5.0, 5.0)
    spread = jnp.exp(jax.random.uniform(keys[1], (WALKERS,), jnp.float32) * math.log(3.0))
    row_factor = jnp.clip(jax.random.normal(keys[2], (4, WALKERS), jnp.float32), -4.0, 4.0)
    col_factor = jnp.clip(0.06 * jax.random.normal(keys[3], (4, PARAMS), jnp.float32), -0.3, 0.3)
    total = spread[:, None] * noise
    for index in range(4):
        total = total + row_factor[index][:, None] * col_factor[index][None, :]
    return total


def place_ends(entries, key, smallest, top_value):
    extent = entries.shape
    index_at = [jax.random.randint(jax.random.fold_in(key, axis), (), 0, extent[axis]) for axis in range(len(extent))]
    entries = entries.at[tuple(index_at)].set(smallest)
    longest = extent.index(max(extent))
    index_at[longest] = (index_at[longest] + 1) % extent[longest]
    return entries.at[tuple(index_at)].set(top_value)


def steps_of(own_key, dims, shards, smallest, largest):
    level = 1.0
    for position, blocks in shards:
        draws = jax.random.uniform(jax.random.fold_in(jax.random.fold_in(own_key, 6), position), (blocks,), jnp.float32, smallest / len(shards), largest / len(shards))
        level = level * jnp.repeat(jnp.exp(draws), dims[position] // blocks).reshape((-1,) + (1,) * (len(dims) - 1 - position))
    return level


def bell_draw(stream_key, dims, scale, bound, cuts=(), kind=jnp.bfloat16):
    drawn = jax.random.normal(stream_key, dims, jnp.float32) * scale
    if len(cuts) > 0:
        drawn = steps_of(stream_key, dims, cuts, -0.22, 0.18) * drawn
    return jnp.clip(drawn, min=-bound, max=bound).astype(kind)


def setup_inputs(seed: int = 0) -> dict:
    key_list = jax.random.split(jax.random.key(seed), 11)
    jacobian = draw_jacobian(jax.random.fold_in(key_list[10], 71), 0)
    prev_update = bell_draw(key_list[1], (N_COL, PARAMS // N_COL), 1.0, 6.0, ((0, 8), (1, 64)), jnp.float32)
    base_energy = bell_draw(key_list[2], (WALKERS,), 1.0, 6.0, ((0, 64),), jnp.float32)
    elec_pos = bell_draw(key_list[3], (WALKERS, 3, NE), 1.5, 8.0, ((0, 64),), jnp.float32)
    atom_pos = bell_draw(key_list[4], (3, NA), 1.5, 6.0, (), jnp.float32)
    quad_ratio = bell_draw(key_list[5], (WALKERS, NA, NE, QUAD), 0.2, 1.2, ((0, 64),), jnp.float32)
    rotation = place_ends(jax.random.randint(key_list[6], (WALKERS, NE), 0, NROT), jax.random.fold_in(key_list[6], 1), 0, NROT - 1).astype(jnp.int32)
    channels = place_ends(jax.random.randint(key_list[7], (NA,), 1, LMAX + 1), jax.random.fold_in(key_list[7], 1), 1, LMAX).astype(jnp.int32)
    ecp_coef = jnp.clip(jax.random.uniform(key_list[8], (NA, LMAX), jnp.float32, 0.5, 2.0), 0.5, 2.0)
    ecp_expo = jnp.clip(jnp.exp(jax.random.uniform(key_list[9], (NA, LMAX), jnp.float32, math.log(0.2), math.log(2.0))), 0.2, 2.0)
    return dict(jacobian=jacobian, prev_update=prev_update, base_energy=base_energy, elec_pos=elec_pos, atom_pos=atom_pos, quad_ratio=quad_ratio, rotation=rotation, channels=channels, ecp_coef=ecp_coef, ecp_expo=ecp_expo)


momentum = 0.9
damping = 0.1

def icosa_points():
    golden = (1.0 + math.sqrt(5.0)) / 2.0
    length = math.sqrt(1.0 + golden * golden)
    rows = []
    for first in (-1.0, 1.0):
        for second in (-golden, golden):
            rows.append((0.0, first / length, second / length))
            rows.append((first / length, second / length, 0.0))
            rows.append((second / length, 0.0, first / length))
    return jnp.asarray(rows, dtype=jnp.float32).T

def rotation_table(count):
    angle = jnp.arange(count, dtype=jnp.float32)
    turn_z = 2.0 * math.pi * angle / count
    turn_x = 0.9 * angle
    cz, sz = (jnp.cos(turn_z), jnp.sin(turn_z))
    cx, sx = (jnp.cos(turn_x), jnp.sin(turn_x))
    zeros = jnp.zeros_like(cz)
    matrix = jnp.stack([jnp.stack([cz, -sz * cx, sz * sx], axis=-1), jnp.stack([sz, cz * cx, -cz * sx], axis=-1), jnp.stack([zeros, sx, cx], axis=-1)], axis=1)
    points = icosa_points()
    rotated = matrix[:, :, 0, None] * points[None, 0, :]
    rotated = rotated + matrix[:, :, 1, None] * points[None, 1, :]
    rotated = rotated + matrix[:, :, 2, None] * points[None, 2, :]
    return rotated.reshape(count, -1)

def nonlocal_energy(elec_pos, atom_pos, quad_ratio, rotation, channels, ecp_coef, ecp_expo):
    walkers, electrons = rotation.shape
    count = NROT
    table = rotation_table(count)
    onehot = (rotation[:, :, None] == jnp.arange(count, dtype=jnp.int32)[None, None, :]).astype(jnp.float32)
    rotated = jnp.einsum('wek,kf->wef', onehot, table, precision=lax.Precision.HIGHEST)
    rotated = rotated.reshape(walkers, electrons, 3, -1)
    diff = elec_pos[:, :, None, :] - atom_pos[None, :, :, None]
    dist2 = lax.optimization_barrier(jnp.sum(diff * diff, axis=1))
    unit = diff / jnp.sqrt(dist2 + 0.01)[:, None, :, :]
    cosang = unit[:, 0, :, :, None] * rotated[:, None, :, 0, :]
    cosang = cosang + unit[:, 1, :, :, None] * rotated[:, None, :, 1, :]
    cosang = cosang + unit[:, 2, :, :, None] * rotated[:, None, :, 2, :]
    quad = quad_ratio.shape[-1]
    lmax = ecp_coef.shape[1]
    lower = jnp.ones_like(cosang)
    upper = cosang
    total = jnp.zeros((walkers,), jnp.float32)
    for level in range(lmax):
        if level == 0:
            poly = lower
        elif level == 1:
            poly = upper
        else:
            fresh = ((2 * level - 1) * cosang * upper - (level - 1) * lower) / level
            lower, upper = (upper, fresh)
            poly = fresh
        angular = lax.optimization_barrier(jnp.sum(poly * quad_ratio, axis=-1)) / quad
        active = (channels > level).astype(jnp.float32)
        radial = ecp_coef[None, :, level, None] * jnp.exp(-ecp_expo[None, :, level, None] * dist2)
        term = (2 * level + 1) * active[None, :, None] * radial * angular
        total = total + lax.optimization_barrier(jnp.sum(term, axis=(1, 2)))
    return total

def reference(jacobian, prev_update, base_energy, elec_pos, atom_pos, quad_ratio, rotation, channels, ecp_coef, ecp_expo):
    local_energy = base_energy + nonlocal_energy(elec_pos, atom_pos, quad_ratio, rotation, channels, ecp_coef, ecp_expo)
    walkers, total = jacobian.shape
    width = math.gcd(total, 8192)
    count = total // width
    means = lax.optimization_barrier(jnp.mean(jacobian, axis=0))
    prev = prev_update.reshape(total)
    scale = 1.0 / total

    def accumulate(index, carry):
        gram, along = carry
        start = (index * width).astype(jnp.int32)
        block = lax.dynamic_slice_in_dim(jacobian, start, width, 1) - lax.dynamic_slice_in_dim(means, start, width, 0)[None, :]
        piece = lax.dynamic_slice_in_dim(prev, start, width, 0)
        gram = gram + jnp.dot(block.astype(jnp.float32), block.T.astype(jnp.float32), precision=lax.Precision.HIGHEST, preferred_element_type=jnp.float32) * scale
        along = along + jnp.dot(block.astype(jnp.float32), piece.astype(jnp.float32), precision=lax.Precision.HIGHEST, preferred_element_type=jnp.float32) * scale
        return (gram, along)
    gram, along = lax.fori_loop(0, count, accumulate, (jnp.zeros((walkers, walkers), jnp.float32), jnp.zeros((walkers,), jnp.float32)))
    eps = -(local_energy - jnp.mean(local_energy)) / math.sqrt(walkers)
    system = gram + damping * jnp.eye(walkers, dtype=jnp.float32)
    factor = jnp.linalg.cholesky(system)
    solved = jax.scipy.linalg.cho_solve((factor, True), eps - momentum * along)

    def project(index):
        start = (index * width).astype(jnp.int32)
        block = lax.dynamic_slice_in_dim(jacobian, start, width, 1) - lax.dynamic_slice_in_dim(means, start, width, 0)[None, :]
        piece = lax.dynamic_slice_in_dim(prev, start, width, 0)
        return jnp.dot(solved.astype(jnp.float32), block.astype(jnp.float32), precision=lax.Precision.HIGHEST, preferred_element_type=jnp.float32) + momentum * piece
    update = lax.map(project, jnp.arange(count, dtype=jnp.int32)).reshape(prev_update.shape)
    return (local_energy, update)
```

```python
import math

import jax
import jax.numpy as jnp
from jax import lax
from jax.experimental import pallas as pl
from jax.experimental.pallas import tpu as pltpu
from jax.sharding import PartitionSpec as P

NROT = 16


momentum = 0.9
damping = 0.1


def icosa_points():
    golden = (1.0 + math.sqrt(5.0)) / 2.0
    length = math.sqrt(1.0 + golden * golden)
    rows = []
    for first in (-1.0, 1.0):
        for second in (-golden, golden):
            rows.append((0.0, first / length, second / length))
            rows.append((first / length, second / length, 0.0))
            rows.append((second / length, 0.0, first / length))
    return jnp.asarray(rows, dtype=jnp.float32).T


def rotation_table(count):
    angle = jnp.arange(count, dtype=jnp.float32)
    turn_z = 2.0 * math.pi * angle / count
    turn_x = 0.9 * angle
    cz, sz = (jnp.cos(turn_z), jnp.sin(turn_z))
    cx, sx = (jnp.cos(turn_x), jnp.sin(turn_x))
    zeros = jnp.zeros_like(cz)
    matrix = jnp.stack(
        [
            jnp.stack([cz, -sz * cx, sz * sx], axis=-1),
            jnp.stack([sz, cz * cx, -cz * sx], axis=-1),
            jnp.stack([zeros, sx, cx], axis=-1),
        ],
        axis=1,
    )
    points = icosa_points()
    rotated = matrix[:, :, 0, None] * points[None, 0, :]
    rotated = rotated + matrix[:, :, 1, None] * points[None, 1, :]
    rotated = rotated + matrix[:, :, 2, None] * points[None, 2, :]
    return rotated.reshape(count, -1)


def nonlocal_energy(elec_pos, atom_pos, quad_ratio, rotation, channels, ecp_coef, ecp_expo):
    walkers, electrons = rotation.shape
    count = NROT
    table = rotation_table(count)
    onehot = (rotation[:, :, None] == jnp.arange(count, dtype=jnp.int32)[None, None, :]).astype(
        jnp.float32
    )
    rotated = jnp.einsum("wek,kf->wef", onehot, table, precision=lax.Precision.HIGHEST)
    rotated = rotated.reshape(walkers, electrons, 3, -1)
    diff = elec_pos[:, :, None, :] - atom_pos[None, :, :, None]
    dist2 = jnp.sum(diff * diff, axis=1)
    unit = diff / jnp.sqrt(dist2 + 0.01)[:, None, :, :]
    cosang = unit[:, 0, :, :, None] * rotated[:, None, :, 0, :]
    cosang = cosang + unit[:, 1, :, :, None] * rotated[:, None, :, 1, :]
    cosang = cosang + unit[:, 2, :, :, None] * rotated[:, None, :, 2, :]
    quad = quad_ratio.shape[-1]
    lmax = ecp_coef.shape[1]
    lower = jnp.ones_like(cosang)
    upper = cosang
    total = jnp.zeros((walkers,), jnp.float32)
    for level in range(lmax):
        if level == 0:
            poly = lower
        elif level == 1:
            poly = upper
        else:
            fresh = ((2 * level - 1) * cosang * upper - (level - 1) * lower) / level
            lower, upper = (upper, fresh)
            poly = fresh
        angular = jnp.sum(poly * quad_ratio, axis=-1) / quad
        active = (channels > level).astype(jnp.float32)
        radial = ecp_coef[None, :, level, None] * jnp.exp(-ecp_expo[None, :, level, None] * dist2)
        term = (2 * level + 1) * active[None, :, None] * radial * angular
        total = total + jnp.sum(term, axis=(1, 2))
    return total


BLOCK = 128
SUB = 8
LANES = 128


def spread_rows(jac_ref, out_ref):
    rows = jac_ref.shape[0]
    for tile in range(jac_ref.shape[1] // LANES):
        owner, sub = divmod(tile, SUB)
        out_ref[pl.ds(owner * rows * SUB + sub, rows, stride=SUB), :] = jac_ref[
            :, tile * LANES : (tile + 1) * LANES
        ]


def dense_pieces(jacobian, owners):
    rows, width = jacobian.shape
    steps = 8
    piece = width // owners
    assert piece == SUB * LANES
    return pl.pallas_call(
        spread_rows,
        grid=(steps,),
        in_specs=[pl.BlockSpec((rows, width // steps), lambda i: (0, i))],
        out_specs=pl.BlockSpec((owners // steps * rows * SUB, LANES), lambda i: (i, 0)),
        out_shape=jax.ShapeDtypeStruct((owners * rows * SUB, LANES), jnp.float32),
        name="dense_pieces",
    )(jacobian)


def split_high_low(value):
    high = value.astype(jnp.bfloat16)
    low = (value - high.astype(jnp.float32)).astype(jnp.bfloat16)
    return high, low


def contract_last(left, right, precision=None):
    return lax.dot_general(
        left,
        right,
        (((1,), (1,)), ((), ())),
        precision=precision,
        preferred_element_type=jnp.float32,
    )


def gram_kernel(scale, x_ref, prev_ref, energy_ref, packed_ref, centred_ref, high_ref, low_ref):
    walkers = centred_ref.shape[0]
    for sub in range(SUB):
        part = x_ref[pl.ds(sub, walkers, stride=SUB), :]
        part = part - jnp.sum(part, axis=0, keepdims=True) * (1.0 / walkers)
        lanes = slice(sub * LANES, (sub + 1) * LANES)
        centred_ref[:, lanes] = part
        high, low = split_high_low(part)
        high_ref[:, lanes] = high
        low_ref[:, lanes] = low
    blocks = walkers // BLOCK
    row = 0
    for i in range(blocks):
        mine = slice(i * BLOCK, (i + 1) * BLOCK)
        rest = slice(i * BLOCK, walkers)
        strip = contract_last(high_ref[mine, :], high_ref[rest, :])
        strip = strip + contract_last(high_ref[mine, :], low_ref[rest, :])
        strip = strip + contract_last(low_ref[mine, :], high_ref[rest, :])
        strip = strip * scale
        for j in range(blocks - i):
            packed_ref[row : row + BLOCK, :] = strip[:, j * BLOCK : (j + 1) * BLOCK]
            row += BLOCK
    along = contract_last(prev_ref[...], centred_ref[...], lax.Precision.HIGHEST) * scale
    packed_ref[row:, :] = jnp.zeros((packed_ref.shape[0] - row, LANES), jnp.float32)
    for j in range(blocks):
        packed_ref[row + j : row + j + 1, :] = along[:, j * BLOCK : (j + 1) * BLOCK]
        packed_ref[row + SUB + j : row + SUB + j + 1, :] = energy_ref[:, j * BLOCK : (j + 1) * BLOCK]


def gram_pieces(received, prev_update, energy_row, walkers, pieces, scale):
    width = prev_update.shape[1]
    return pl.pallas_call(
        lambda *refs: gram_kernel(scale, *refs),
        out_shape=(
            jax.ShapeDtypeStruct((pieces * BLOCK, LANES), jnp.float32),
            jax.ShapeDtypeStruct((walkers, width), jnp.float32),
        ),
        scratch_shapes=[
            pltpu.VMEM((walkers, width), jnp.bfloat16),
            pltpu.VMEM((walkers, width), jnp.bfloat16),
        ],
        name="gram_pieces",
    )(received, prev_update, energy_row)


def body(
    jacobian,
    prev_update,
    base_energy,
    elec_pos,
    atom_pos,
    quad_ratio,
    rotation,
    channels,
    ecp_coef,
    ecp_expo,
):
    owners = lax.axis_size("walk")
    columns = lax.axis_size("col")
    rows, width = jacobian.shape
    walkers = rows * owners
    scale = 1.0 / (width * columns)
    pieces = dense_pieces(jacobian, owners).reshape(owners, rows * SUB, LANES)
    received = lax.all_to_all(pieces, "walk", split_axis=0, concat_axis=0, tiled=True)
    energy_mine = base_energy + nonlocal_energy(
        elec_pos, atom_pos, quad_ratio, rotation, channels, ecp_coef, ecp_expo
    )
    energy_row = lax.dynamic_update_slice(
        jnp.zeros((walkers,), jnp.float32), energy_mine / columns, (lax.axis_index("walk") * rows,)
    )
    packed, centred = gram_pieces(
        received.reshape(walkers * SUB, LANES),
        prev_update,
        energy_row[None, :],
        walkers,
        columns,
        scale,
    )
    shares = lax.all_to_all(
        packed.reshape(columns, BLOCK, LANES), "col", split_axis=0, concat_axis=0, tiled=True
    )
    share = jnp.sum(shares, axis=0).reshape(owners, -1, LANES)
    cells = lax.all_to_all(share, "walk", split_axis=0, concat_axis=0, tiled=True)
    cell = jnp.sum(cells, axis=0)
    full = lax.all_to_all(
        jnp.broadcast_to(cell[None], cells.shape), "walk", split_axis=0, concat_axis=0, tiled=True
    )
    whole = lax.all_gather(full.reshape(BLOCK, LANES), "col", axis=0, tiled=False)
    along = whole[6, 0:3].reshape(walkers)
    energies = whole[6, SUB : SUB + 3].reshape(walkers)
    gram = jnp.concatenate(
        [
            jnp.concatenate([whole[0], whole[1], whole[2]], axis=1),
            jnp.concatenate([whole[1].T, whole[3], whole[4]], axis=1),
            jnp.concatenate([whole[2].T, whole[4].T, whole[5]], axis=1),
        ],
        axis=0,
    )
    eps = -(energies - jnp.mean(energies)) / math.sqrt(walkers)
    system = gram + damping * jnp.eye(walkers, dtype=jnp.float32)
    factor = jnp.linalg.cholesky(system)
    solved = jax.scipy.linalg.cho_solve((factor, True), eps - momentum * along)
    update_mine = (
        jnp.dot(
            solved, centred, precision=lax.Precision.HIGHEST, preferred_element_type=jnp.float32
        )
        + momentum * prev_update[0]
    )
    return (energy_mine, update_mine[None, :])


def solution(mesh):
    in_specs = (
        P("walk", "col"),
        P("col", "walk"),
        P("walk"),
        P("walk", None, None),
        P(),
        P("walk", None, None, None),
        P("walk", None),
        P(),
        P(),
        P(),
    )
    out_specs = (P("walk"), P("col", "walk"))
    return jax.shard_map(body, mesh=mesh, in_specs=in_specs, out_specs=out_specs, check_vma=False)
```

```python
import math

import jax
import jax.numpy as jnp
from jax import lax
from jax.experimental import pallas as pl
from jax.experimental.pallas import tpu as pltpu
from jax.sharding import PartitionSpec as P

NROT = 16


momentum = 0.9
damping = 0.1


def icosa_points():
    golden = (1.0 + math.sqrt(5.0)) / 2.0
    length = math.sqrt(1.0 + golden * golden)
    rows = []
    for first in (-1.0, 1.0):
        for second in (-golden, golden):
            rows.append((0.0, first / length, second / length))
            rows.append((first / length, second / length, 0.0))
            rows.append((second / length, 0.0, first / length))
    return jnp.asarray(rows, dtype=jnp.float32).T


def rotation_table(count):
    angle = jnp.arange(count, dtype=jnp.float32)
    turn_z = 2.0 * math.pi * angle / count
    turn_x = 0.9 * angle
    cz, sz = (jnp.cos(turn_z), jnp.sin(turn_z))
    cx, sx = (jnp.cos(turn_x), jnp.sin(turn_x))
    zeros = jnp.zeros_like(cz)
    matrix = jnp.stack(
        [
            jnp.stack([cz, -sz * cx, sz * sx], axis=-1),
            jnp.stack([sz, cz * cx, -cz * sx], axis=-1),
            jnp.stack([zeros, sx, cx], axis=-1),
        ],
        axis=1,
    )
    points = icosa_points()
    rotated = matrix[:, :, 0, None] * points[None, 0, :]
    rotated = rotated + matrix[:, :, 1, None] * points[None, 1, :]
    rotated = rotated + matrix[:, :, 2, None] * points[None, 2, :]
    return rotated.reshape(count, -1)


def nonlocal_energy(elec_pos, atom_pos, quad_ratio, rotation, channels, ecp_coef, ecp_expo):
    walkers, electrons = rotation.shape
    count = NROT
    table = rotation_table(count)
    onehot = (rotation[:, :, None] == jnp.arange(count, dtype=jnp.int32)[None, None, :]).astype(
        jnp.float32
    )
    rotated = jnp.einsum("wek,kf->wef", onehot, table, precision=lax.Precision.HIGHEST)
    rotated = rotated.reshape(walkers, electrons, 3, -1)
    diff = elec_pos[:, :, None, :] - atom_pos[None, :, :, None]
    dist2 = jnp.sum(diff * diff, axis=1)
    unit = diff / jnp.sqrt(dist2 + 0.01)[:, None, :, :]
    cosang = unit[:, 0, :, :, None] * rotated[:, None, :, 0, :]
    cosang = cosang + unit[:, 1, :, :, None] * rotated[:, None, :, 1, :]
    cosang = cosang + unit[:, 2, :, :, None] * rotated[:, None, :, 2, :]
    quad = quad_ratio.shape[-1]
    lmax = ecp_coef.shape[1]
    lower = jnp.ones_like(cosang)
    upper = cosang
    total = jnp.zeros((walkers,), jnp.float32)
    for level in range(lmax):
        if level == 0:
            poly = lower
        elif level == 1:
            poly = upper
        else:
            fresh = ((2 * level - 1) * cosang * upper - (level - 1) * lower) / level
            lower, upper = (upper, fresh)
            poly = fresh
        angular = jnp.sum(poly * quad_ratio, axis=-1) / quad
        active = (channels > level).astype(jnp.float32)
        radial = ecp_coef[None, :, level, None] * jnp.exp(-ecp_expo[None, :, level, None] * dist2)
        term = (2 * level + 1) * active[None, :, None] * radial * angular
        total = total + jnp.sum(term, axis=(1, 2))
    return total


BLOCK = 128
SUB = 8
LANES = 128


def spread_rows(jac_ref, out_ref):
    rows = jac_ref.shape[0]
    for tile in range(jac_ref.shape[1] // LANES):
        owner, sub = divmod(tile, SUB)
        out_ref[pl.ds(owner * rows * SUB + sub, rows, stride=SUB), :] = jac_ref[
            :, tile * LANES : (tile + 1) * LANES
        ]


def dense_pieces(jacobian, owners):
    rows, width = jacobian.shape
    steps = 8
    piece = width // owners
    assert piece == SUB * LANES
    return pl.pallas_call(
        spread_rows,
        grid=(steps,),
        in_specs=[pl.BlockSpec((rows, width // steps), lambda i: (0, i))],
        out_specs=pl.BlockSpec((owners // steps * rows * SUB, LANES), lambda i: (i, 0)),
        out_shape=jax.ShapeDtypeStruct((owners * rows * SUB, LANES), jnp.float32),
        name="dense_pieces",
    )(jacobian)


def split_high_low(value):
    high = value.astype(jnp.bfloat16)
    low = (value - high.astype(jnp.float32)).astype(jnp.bfloat16)
    return high, low


def contract_last(left, right, precision=None):
    return lax.dot_general(
        left,
        right,
        (((1,), (1,)), ((), ())),
        precision=precision,
        preferred_element_type=jnp.float32,
    )


def gram_kernel(scale, x_ref, prev_ref, energy_ref, packed_ref, centred_ref, high_ref, low_ref):
    walkers = centred_ref.shape[0]
    for sub in range(SUB):
        part = x_ref[pl.ds(sub, walkers, stride=SUB), :]
        part = part - jnp.sum(part, axis=0, keepdims=True) * (1.0 / walkers)
        lanes = slice(sub * LANES, (sub + 1) * LANES)
        centred_ref[:, lanes] = part
        high, low = split_high_low(part)
        high_ref[:, lanes] = high
        low_ref[:, lanes] = low
    blocks = walkers // BLOCK
    row = 0
    for i in range(blocks):
        mine = slice(i * BLOCK, (i + 1) * BLOCK)
        rest = slice(i * BLOCK, walkers)
        strip = contract_last(high_ref[mine, :], high_ref[rest, :])
        strip = strip + contract_last(high_ref[mine, :], low_ref[rest, :])
        strip = strip + contract_last(low_ref[mine, :], high_ref[rest, :])
        strip = strip * scale
        for j in range(blocks - i):
            packed_ref[row : row + BLOCK, :] = strip[:, j * BLOCK : (j + 1) * BLOCK]
            row += BLOCK
    along = contract_last(prev_ref[...], centred_ref[...], lax.Precision.HIGHEST) * scale
    packed_ref[row:, :] = jnp.zeros((packed_ref.shape[0] - row, LANES), jnp.float32)
    for j in range(blocks):
        packed_ref[row + j : row + j + 1, :] = along[:, j * BLOCK : (j + 1) * BLOCK]
        packed_ref[row + SUB + j : row + SUB + j + 1, :] = energy_ref[:, j * BLOCK : (j + 1) * BLOCK]


def gram_pieces(received, prev_update, energy_row, walkers, pieces, scale):
    width = prev_update.shape[1]
    return pl.pallas_call(
        lambda *refs: gram_kernel(scale, *refs),
        in_specs=[pl.BlockSpec(memory_space=pltpu.VMEM)] * 3,
        out_specs=[pl.BlockSpec(memory_space=pltpu.VMEM)] * 2,
        out_shape=(
            jax.ShapeDtypeStruct((pieces * BLOCK, LANES), jnp.float32),
            jax.ShapeDtypeStruct((walkers, width), jnp.float32),
        ),
        scratch_shapes=[
            pltpu.VMEM((walkers, width), jnp.bfloat16),
            pltpu.VMEM((walkers, width), jnp.bfloat16),
        ],
        name="gram_pieces",
    )(received, prev_update, energy_row)


def matmul(left, right, left_dim=1, right_dim=0):
    return lax.dot_general(
        left,
        right,
        (((left_dim,), (right_dim,)), ((), ())),
        precision=lax.Precision.HIGHEST,
        preferred_element_type=jnp.float32,
    )


def inverse(block):
    lane = lax.broadcasted_iota(jnp.int32, (SUB, BLOCK), 1)
    row_of = lax.broadcasted_iota(jnp.int32, (SUB, BLOCK), 0)
    lane_rest = lax.broadcasted_iota(jnp.int32, (BLOCK - SUB, BLOCK), 1)
    full = (SUB, BLOCK)

    def step(_, value):
        panel, rest = value[:SUB], value[SUB:]
        columns = [rest[:, k : k + 1] for k in range(SUB)]
        pivots = [jnp.broadcast_to(panel[:, k : k + 1], full) for k in range(SUB)]
        for k in range(SUB):
            column = pivots[k]
            scale = 1.0 / jnp.broadcast_to(column[k : k + 1, :], full)
            mine = row_of == k
            row = jnp.broadcast_to(panel[k : k + 1, :], full)
            row = jnp.where(lane == k, scale, row * scale)
            panel = jnp.where(mine, row, jnp.where(lane == k, 0.0, panel) - column * row)
            for j in range(k + 1, SUB):
                other = jnp.broadcast_to(pivots[j][k : k + 1, :], full) * scale
                pivots[j] = jnp.where(mine, other, pivots[j] - column * other)
        rest = jnp.where(lane_rest < SUB, 0.0, rest)
        for k in range(SUB):
            rest = rest - columns[k] * panel[k : k + 1, :]
        return pltpu.roll(jnp.concatenate([rest, panel], axis=0), BLOCK - SUB, 1)

    return lax.fori_loop(0, BLOCK // SUB, step, block)


def solve_kernel(whole_ref, centred_ref, prev_ref, out_ref):
    lane = lax.broadcasted_iota(jnp.int32, (BLOCK, BLOCK), 1)
    row_of = lax.broadcasted_iota(jnp.int32, (BLOCK, BLOCK), 0)
    shift = jnp.where(lane == row_of, damping, 0.0)
    walkers = centred_ref.shape[0]

    def gram(index):
        return whole_ref[index * BLOCK : (index + 1) * BLOCK, :]

    along = [whole_ref[6 * BLOCK + j : 6 * BLOCK + j + 1, :] for j in range(3)]
    energies = [whole_ref[6 * BLOCK + SUB + j : 6 * BLOCK + SUB + j + 1, :] for j in range(3)]
    mean = sum(jnp.sum(part, axis=1, keepdims=True) for part in energies) * (1.0 / walkers)
    right = [
        (mean - energy) * (1.0 / math.sqrt(walkers)) - momentum * part
        for energy, part in zip(energies, along)
    ]
    g01, g02, g12 = gram(1), gram(2), gram(4)
    inv0 = inverse(gram(0) + shift)
    w01, w02 = matmul(inv0, g01), matmul(inv0, g02)
    s11 = gram(3) + shift - matmul(g01, w01, 0, 0)
    s12 = g12 - matmul(g01, w02, 0, 0)
    s22 = gram(5) + shift - matmul(g02, w02, 0, 0)
    y0 = matmul(right[0], inv0)
    r1 = right[1] - matmul(y0, g01)
    r2 = right[2] - matmul(y0, g02)
    inv1 = inverse(s11)
    w12 = matmul(inv1, s12)
    s22 = s22 - matmul(s12, w12, 0, 0)
    y1 = matmul(r1, inv1)
    r2 = r2 - matmul(y1, s12)
    inv2 = inverse(s22)
    x2 = matmul(r2, inv2)
    x1 = y1 - matmul(x2, w12, 1, 1)
    x0 = y0 - matmul(x1, w01, 1, 1) - matmul(x2, w02, 1, 1)
    out_ref[...] = (
        matmul(x0, centred_ref[0:BLOCK, :])
        + matmul(x1, centred_ref[BLOCK : 2 * BLOCK, :])
        + matmul(x2, centred_ref[2 * BLOCK :, :])
        + momentum * prev_ref[...]
    )


def solve_update(whole, centred, prev_update):
    return pl.pallas_call(
        solve_kernel,
        in_specs=[pl.BlockSpec(memory_space=pltpu.VMEM)] * 3,
        out_specs=pl.BlockSpec(memory_space=pltpu.VMEM),
        out_shape=jax.ShapeDtypeStruct(prev_update.shape, jnp.float32),
        name="solve_update",
    )(whole, centred, prev_update)


def body(
    jacobian,
    prev_update,
    base_energy,
    elec_pos,
    atom_pos,
    quad_ratio,
    rotation,
    channels,
    ecp_coef,
    ecp_expo,
):
    owners = lax.axis_size("walk")
    columns = lax.axis_size("col")
    rows, width = jacobian.shape
    walkers = rows * owners
    scale = 1.0 / (width * columns)
    pieces = dense_pieces(jacobian, owners).reshape(owners, rows * SUB, LANES)
    received = lax.all_to_all(pieces, "walk", split_axis=0, concat_axis=0, tiled=True)
    energy_mine = base_energy + nonlocal_energy(
        elec_pos, atom_pos, quad_ratio, rotation, channels, ecp_coef, ecp_expo
    )
    energy_row = lax.dynamic_update_slice(
        jnp.zeros((walkers,), jnp.float32), energy_mine / columns, (lax.axis_index("walk") * rows,)
    )
    packed, centred = gram_pieces(
        received.reshape(walkers * SUB, LANES),
        prev_update,
        energy_row[None, :],
        walkers,
        columns,
        scale,
    )
    shares = lax.all_to_all(
        packed.reshape(columns, BLOCK, LANES), "col", split_axis=0, concat_axis=0, tiled=True
    )
    share = jnp.sum(shares, axis=0).reshape(owners, -1, LANES)
    cells = lax.all_to_all(share, "walk", split_axis=0, concat_axis=0, tiled=True)
    cell = jnp.sum(cells, axis=0)
    full = lax.all_to_all(
        jnp.broadcast_to(cell[None], cells.shape), "walk", split_axis=0, concat_axis=0, tiled=True
    )
    whole = lax.all_gather(full.reshape(BLOCK, LANES), "col", axis=0, tiled=False)
    update_mine = solve_update(whole.reshape(columns * BLOCK, LANES), centred, prev_update)
    return (energy_mine, update_mine)


def solution(mesh):
    in_specs = (
        P("walk", "col"),
        P("col", "walk"),
        P("walk"),
        P("walk", None, None),
        P(),
        P("walk", None, None, None),
        P("walk", None),
        P(),
        P(),
        P(),
    )
    out_specs = (P("walk"), P("col", "walk"))
    return jax.shard_map(body, mesh=mesh, in_specs=in_specs, out_specs=out_specs, check_vma=False)
```

```python
import math

import jax
import jax.numpy as jnp
from jax import lax
from jax.experimental import pallas as pl
from jax.experimental.pallas import tpu as pltpu
from jax.sharding import PartitionSpec as P

NROT = 16


momentum = 0.9
damping = 0.1


def icosa_points():
    golden = (1.0 + math.sqrt(5.0)) / 2.0
    length = math.sqrt(1.0 + golden * golden)
    rows = []
    for first in (-1.0, 1.0):
        for second in (-golden, golden):
            rows.append((0.0, first / length, second / length))
            rows.append((first / length, second / length, 0.0))
            rows.append((second / length, 0.0, first / length))
    return jnp.asarray(rows, dtype=jnp.float32).T


def rotation_table(count):
    angle = jnp.arange(count, dtype=jnp.float32)
    turn_z = 2.0 * math.pi * angle / count
    turn_x = 0.9 * angle
    cz, sz = (jnp.cos(turn_z), jnp.sin(turn_z))
    cx, sx = (jnp.cos(turn_x), jnp.sin(turn_x))
    zeros = jnp.zeros_like(cz)
    matrix = jnp.stack(
        [
            jnp.stack([cz, -sz * cx, sz * sx], axis=-1),
            jnp.stack([sz, cz * cx, -cz * sx], axis=-1),
            jnp.stack([zeros, sx, cx], axis=-1),
        ],
        axis=1,
    )
    points = icosa_points()
    rotated = matrix[:, :, 0, None] * points[None, 0, :]
    rotated = rotated + matrix[:, :, 1, None] * points[None, 1, :]
    rotated = rotated + matrix[:, :, 2, None] * points[None, 2, :]
    return rotated.reshape(count, -1)


def nonlocal_energy(elec_pos, atom_pos, quad_ratio, rotation, channels, ecp_coef, ecp_expo):
    walkers, electrons = rotation.shape
    count = NROT
    table = rotation_table(count)
    onehot = (rotation[:, :, None] == jnp.arange(count, dtype=jnp.int32)[None, None, :]).astype(
        jnp.float32
    )
    rotated = jnp.einsum("wek,kf->wef", onehot, table, precision=lax.Precision.HIGHEST)
    rotated = rotated.reshape(walkers, electrons, 3, -1)
    diff = elec_pos[:, :, None, :] - atom_pos[None, :, :, None]
    dist2 = jnp.sum(diff * diff, axis=1)
    unit = diff / jnp.sqrt(dist2 + 0.01)[:, None, :, :]
    cosang = unit[:, 0, :, :, None] * rotated[:, None, :, 0, :]
    cosang = cosang + unit[:, 1, :, :, None] * rotated[:, None, :, 1, :]
    cosang = cosang + unit[:, 2, :, :, None] * rotated[:, None, :, 2, :]
    quad = quad_ratio.shape[-1]
    lmax = ecp_coef.shape[1]
    lower = jnp.ones_like(cosang)
    upper = cosang
    total = jnp.zeros((walkers,), jnp.float32)
    for level in range(lmax):
        if level == 0:
            poly = lower
        elif level == 1:
            poly = upper
        else:
            fresh = ((2 * level - 1) * cosang * upper - (level - 1) * lower) / level
            lower, upper = (upper, fresh)
            poly = fresh
        angular = jnp.sum(poly * quad_ratio, axis=-1) / quad
        active = (channels > level).astype(jnp.float32)
        radial = ecp_coef[None, :, level, None] * jnp.exp(-ecp_expo[None, :, level, None] * dist2)
        term = (2 * level + 1) * active[None, :, None] * radial * angular
        total = total + jnp.sum(term, axis=(1, 2))
    return total


BLOCK = 128
HALF = 64
SUB = 8
LANES = 128
WALK = ("z", "y")
COL = ("x", "core")
PLANE = ("core", "x", "y")


def spread_rows(jac_ref, out_ref):
    rows = jac_ref.shape[0]
    for tile in range(jac_ref.shape[1] // LANES):
        owner, sub = divmod(tile, SUB)
        out_ref[pl.ds(owner * rows * SUB + sub, rows, stride=SUB), :] = jac_ref[
            :, tile * LANES : (tile + 1) * LANES
        ]


def dense_pieces(jacobian, owners):
    rows, width = jacobian.shape
    steps = 2
    piece = width // owners
    assert piece == SUB * LANES
    return pl.pallas_call(
        spread_rows,
        grid=(steps,),
        in_specs=[pl.BlockSpec((rows, width // steps), lambda i: (0, i))],
        out_specs=pl.BlockSpec((owners // steps * rows * SUB, LANES), lambda i: (i, 0)),
        out_shape=jax.ShapeDtypeStruct((owners * rows * SUB, LANES), jnp.float32),
        name="dense_pieces",
    )(jacobian)


def split_high_low(value):
    high = value.astype(jnp.bfloat16)
    low = (value - high.astype(jnp.float32)).astype(jnp.bfloat16)
    return high, low


def contract_last(left, right, precision=None):
    return lax.dot_general(
        left,
        right,
        (((1,), (1,)), ((), ())),
        precision=precision,
        preferred_element_type=jnp.float32,
    )


def gram_kernel(scale, x_ref, prev_ref, energy_ref, packed_ref, centred_ref, high_ref, low_ref):
    walkers = centred_ref.shape[0]
    for sub in range(SUB):
        part = x_ref[pl.ds(sub, walkers, stride=SUB), :]
        part = part - jnp.sum(part, axis=0, keepdims=True) * (1.0 / walkers)
        lanes = slice(sub * LANES, (sub + 1) * LANES)
        centred_ref[:, lanes] = part
        high, low = split_high_low(part)
        high_ref[:, lanes] = high
        low_ref[:, lanes] = low
    blocks = walkers // BLOCK
    row = 0
    for i in range(blocks):
        mine = slice(i * BLOCK, (i + 1) * BLOCK)
        rest = slice(i * BLOCK, walkers)
        strip = contract_last(high_ref[mine, :], high_ref[rest, :])
        strip = strip + contract_last(high_ref[mine, :], low_ref[rest, :])
        strip = strip + contract_last(low_ref[mine, :], high_ref[rest, :])
        strip = strip * scale
        for j in range(blocks - i):
            packed_ref[row : row + BLOCK, :] = strip[:, j * BLOCK : (j + 1) * BLOCK]
            row += BLOCK
    along = contract_last(prev_ref[...], centred_ref[...], lax.Precision.HIGHEST) * scale
    for j in range(walkers // HALF):
        part = slice(j * HALF, (j + 1) * HALF)
        packed_ref[HALF + j : HALF + j + 1, :HALF] = along[:, part]
        packed_ref[HALF + SUB + j : HALF + SUB + j + 1, :HALF] = energy_ref[:, part]


def gram_pieces(received, prev_update, energy_row, walkers, scale):
    width = prev_update.shape[1]
    blocks = walkers // BLOCK
    pieces = blocks * (blocks + 1) // 2
    return pl.pallas_call(
        lambda *refs: gram_kernel(scale, *refs),
        in_specs=[pl.BlockSpec(memory_space=pltpu.VMEM)] * 3,
        out_specs=[pl.BlockSpec(memory_space=pltpu.VMEM)] * 2,
        out_shape=(
            pltpu.VMEM((pieces * BLOCK, LANES), jnp.float32),
            pltpu.VMEM((walkers, width), jnp.float32),
        ),
        scratch_shapes=[
            pltpu.VMEM((walkers, width), jnp.bfloat16),
            pltpu.VMEM((walkers, width), jnp.bfloat16),
        ],
        name="gram_pieces",
    )(received, prev_update, energy_row)


def near(value):
    return pltpu.with_memory_space_constraint(value, pltpu.VMEM)


def matmul(left, right, left_dim=1, right_dim=0):
    return lax.dot_general(
        left,
        right,
        (((left_dim,), (right_dim,)), ((), ())),
        precision=lax.Precision.HIGHEST,
        preferred_element_type=jnp.float32,
    )


def inverse(block):
    lane = lax.broadcasted_iota(jnp.int32, (SUB, BLOCK), 1)
    row_of = lax.broadcasted_iota(jnp.int32, (SUB, BLOCK), 0)
    lane_rest = lax.broadcasted_iota(jnp.int32, (BLOCK - SUB, BLOCK), 1)
    full = (SUB, BLOCK)

    def step(_, value):
        panel, rest = value[:SUB], value[SUB:]
        columns = [rest[:, k : k + 1] for k in range(SUB)]
        pivots = [jnp.broadcast_to(panel[:, k : k + 1], full) for k in range(SUB)]
        for k in range(SUB):
            column = pivots[k]
            scale = 1.0 / jnp.broadcast_to(column[k : k + 1, :], full)
            mine = row_of == k
            row = jnp.broadcast_to(panel[k : k + 1, :], full)
            row = jnp.where(lane == k, scale, row * scale)
            panel = jnp.where(mine, row, jnp.where(lane == k, 0.0, panel) - column * row)
            for j in range(k + 1, SUB):
                other = jnp.broadcast_to(pivots[j][k : k + 1, :], full) * scale
                pivots[j] = jnp.where(mine, other, pivots[j] - column * other)
        rest = jnp.where(lane_rest < SUB, 0.0, rest)
        for k in range(SUB):
            rest = rest - columns[k] * panel[k : k + 1, :]
        return pltpu.roll(jnp.concatenate([rest, panel], axis=0), BLOCK - SUB, 1)

    return lax.fori_loop(0, BLOCK // SUB, step, block)


def solve_kernel(whole_ref, centred_ref, prev_ref, out_ref):
    lane = lax.broadcasted_iota(jnp.int32, (BLOCK, BLOCK), 1)
    row_of = lax.broadcasted_iota(jnp.int32, (BLOCK, BLOCK), 0)
    shift = jnp.where(lane == row_of, damping, 0.0)
    walkers = centred_ref.shape[0]

    def gram(index):
        return whole_ref[index * BLOCK : (index + 1) * BLOCK, :]

    def vector(first):
        halves = [whole_ref[first + j : first + j + 1, :HALF] for j in range(walkers // HALF)]
        return [jnp.concatenate(halves[j : j + 2], axis=1) for j in range(0, len(halves), 2)]

    along = vector(HALF)
    energies = vector(HALF + SUB)
    corner = whole_ref[:HALF, HALF:BLOCK].T
    lower = jnp.concatenate([corner, whole_ref[HALF:BLOCK, HALF:BLOCK]], axis=1)
    g00 = jnp.concatenate([whole_ref[:HALF, :], lower], axis=0)
    mean = sum(jnp.sum(part, axis=1, keepdims=True) for part in energies) * (1.0 / walkers)
    right = [
        (mean - energy) * (1.0 / math.sqrt(walkers)) - momentum * part
        for energy, part in zip(energies, along)
    ]
    g01, g02, g12 = gram(1), gram(2), gram(4)
    inv0 = inverse(g00 + shift)
    w01, w02 = matmul(inv0, g01), matmul(inv0, g02)
    s11 = gram(3) + shift - matmul(g01, w01, 0, 0)
    s12 = g12 - matmul(g01, w02, 0, 0)
    s22 = gram(5) + shift - matmul(g02, w02, 0, 0)
    y0 = matmul(right[0], inv0)
    r1 = right[1] - matmul(y0, g01)
    r2 = right[2] - matmul(y0, g02)
    inv1 = inverse(s11)
    w12 = matmul(inv1, s12)
    s22 = s22 - matmul(s12, w12, 0, 0)
    y1 = matmul(r1, inv1)
    r2 = r2 - matmul(y1, s12)
    inv2 = inverse(s22)
    x2 = matmul(r2, inv2)
    x1 = y1 - matmul(x2, w12, 1, 1)
    x0 = y0 - matmul(x1, w01, 1, 1) - matmul(x2, w02, 1, 1)
    out_ref[...] = (
        matmul(x0, centred_ref[0:BLOCK, :])
        + matmul(x1, centred_ref[BLOCK : 2 * BLOCK, :])
        + matmul(x2, centred_ref[2 * BLOCK :, :])
        + momentum * prev_ref[...]
    )


def solve_update(whole, centred, prev_update):
    return pl.pallas_call(
        solve_kernel,
        in_specs=[pl.BlockSpec(memory_space=pltpu.VMEM)] * 3,
        out_specs=pl.BlockSpec(memory_space=pltpu.VMEM),
        out_shape=jax.ShapeDtypeStruct(prev_update.shape, jnp.float32),
        name="solve_update",
    )(whole, centred, prev_update)


def exchange(pieces, axes):
    return lax.all_to_all(pieces, axes, split_axis=0, concat_axis=0, tiled=True)


def hand_round(value, axes):
    return exchange(jnp.broadcast_to(value[None], (lax.axis_size(axes), *value.shape)), axes)


def body(
    jacobian,
    prev_update,
    base_energy,
    elec_pos,
    atom_pos,
    quad_ratio,
    rotation,
    channels,
    ecp_coef,
    ecp_expo,
):
    owners = lax.axis_size(WALK)
    columns = lax.axis_size(COL)
    rows, width = jacobian.shape
    walkers = rows * owners
    scale = 1.0 / (width * columns)
    energy_mine = base_energy + nonlocal_energy(
        elec_pos, atom_pos, quad_ratio, rotation, channels, ecp_coef, ecp_expo
    )
    energy_row = lax.dynamic_update_slice(
        jnp.zeros((1, walkers), jnp.float32),
        energy_mine[None, :] / columns,
        (0, lax.axis_index(WALK) * rows),
    )
    pieces = dense_pieces(jacobian, owners).reshape(owners, rows * SUB, LANES)
    pieces, energy_row = lax.optimization_barrier((pieces, energy_row))
    received = exchange(pieces, WALK)
    packed, centred = gram_pieces(
        near(received.reshape(walkers * SUB, LANES)), prev_update, near(energy_row), walkers, scale
    )
    plane = lax.axis_size(PLANE)
    share = jnp.sum(exchange(packed.reshape(plane, -1, LANES), PLANE), axis=0)
    share = jnp.sum(hand_round(share, "z"), axis=0)
    whole = hand_round(share, PLANE)
    update_mine = solve_update(near(whole.reshape(packed.shape)), near(centred), prev_update)
    return (energy_mine, update_mine)


def solution(mesh):
    mesh = jax.sharding.Mesh(mesh.devices.reshape(16, 4, 4, 2), ("z", "y", "x", "core"))
    in_specs = (
        P(WALK, COL),
        P(COL, WALK),
        P(WALK),
        P(WALK, None, None),
        P(),
        P(WALK, None, None, None),
        P(WALK, None),
        P(),
        P(),
        P(),
    )
    out_specs = (P(WALK), P(COL, WALK))
    return jax.shard_map(body, mesh=mesh, in_specs=in_specs, out_specs=out_specs, check_vma=False)
```

```python
import math

import jax
import jax.numpy as jnp
from jax import lax
from jax.experimental import pallas as pl
from jax.experimental.pallas import tpu as pltpu
from jax.sharding import PartitionSpec as P

NROT = 16


momentum = 0.9
damping = 0.1


def icosa_points():
    golden = (1.0 + math.sqrt(5.0)) / 2.0
    length = math.sqrt(1.0 + golden * golden)
    rows = []
    for first in (-1.0, 1.0):
        for second in (-golden, golden):
            rows.append((0.0, first / length, second / length))
            rows.append((first / length, second / length, 0.0))
            rows.append((second / length, 0.0, first / length))
    return jnp.asarray(rows, dtype=jnp.float32).T


def rotation_table(count):
    angle = jnp.arange(count, dtype=jnp.float32)
    turn_z = 2.0 * math.pi * angle / count
    turn_x = 0.9 * angle
    cz, sz = (jnp.cos(turn_z), jnp.sin(turn_z))
    cx, sx = (jnp.cos(turn_x), jnp.sin(turn_x))
    zeros = jnp.zeros_like(cz)
    matrix = jnp.stack(
        [
            jnp.stack([cz, -sz * cx, sz * sx], axis=-1),
            jnp.stack([sz, cz * cx, -cz * sx], axis=-1),
            jnp.stack([zeros, sx, cx], axis=-1),
        ],
        axis=1,
    )
    points = icosa_points()
    rotated = matrix[:, :, 0, None] * points[None, 0, :]
    rotated = rotated + matrix[:, :, 1, None] * points[None, 1, :]
    rotated = rotated + matrix[:, :, 2, None] * points[None, 2, :]
    return rotated.reshape(count, -1)


def nonlocal_energy(elec_pos, atom_pos, quad_ratio, rotation, channels, ecp_coef, ecp_expo):
    walkers, electrons = rotation.shape
    count = NROT
    table = rotation_table(count)
    onehot = (rotation[:, :, None] == jnp.arange(count, dtype=jnp.int32)[None, None, :]).astype(
        jnp.float32
    )
    rotated = jnp.einsum("wek,kf->wef", onehot, table, precision=lax.Precision.HIGHEST)
    rotated = rotated.reshape(walkers, electrons, 3, -1)
    diff = elec_pos[:, :, None, :] - atom_pos[None, :, :, None]
    dist2 = jnp.sum(diff * diff, axis=1)
    unit = diff / jnp.sqrt(dist2 + 0.01)[:, None, :, :]
    cosang = unit[:, 0, :, :, None] * rotated[:, None, :, 0, :]
    cosang = cosang + unit[:, 1, :, :, None] * rotated[:, None, :, 1, :]
    cosang = cosang + unit[:, 2, :, :, None] * rotated[:, None, :, 2, :]
    quad = quad_ratio.shape[-1]
    lmax = ecp_coef.shape[1]
    lower = jnp.ones_like(cosang)
    upper = cosang
    total = jnp.zeros((walkers,), jnp.float32)
    for level in range(lmax):
        if level == 0:
            poly = lower
        elif level == 1:
            poly = upper
        else:
            fresh = ((2 * level - 1) * cosang * upper - (level - 1) * lower) / level
            lower, upper = (upper, fresh)
            poly = fresh
        angular = jnp.sum(poly * quad_ratio, axis=-1) / quad
        active = (channels > level).astype(jnp.float32)
        radial = ecp_coef[None, :, level, None] * jnp.exp(-ecp_expo[None, :, level, None] * dist2)
        term = (2 * level + 1) * active[None, :, None] * radial * angular
        total = total + jnp.sum(term, axis=(1, 2))
    return total


BLOCK = 128
HALF = 64
SUB = 8
LANES = 128
WALK = ("z", "y")
COL = ("x", "core")
PLANE = ("core", "x", "y")


def spread_rows(jac_ref, out_ref):
    rows = jac_ref.shape[0]
    for tile in range(jac_ref.shape[1] // LANES):
        owner, sub = divmod(tile, SUB)
        out_ref[pl.ds(owner * rows * SUB + sub, rows, stride=SUB), :] = jac_ref[
            :, tile * LANES : (tile + 1) * LANES
        ]


def dense_pieces(jacobian, owners):
    rows, width = jacobian.shape
    steps = 2
    piece = width // owners
    assert piece == SUB * LANES
    return pl.pallas_call(
        spread_rows,
        grid=(steps,),
        in_specs=[pl.BlockSpec((rows, width // steps), lambda i: (0, i))],
        out_specs=pl.BlockSpec((owners // steps * rows * SUB, LANES), lambda i: (i, 0)),
        out_shape=jax.ShapeDtypeStruct((owners * rows * SUB, LANES), jnp.float32),
        name="dense_pieces",
    )(jacobian)


def split_high_low(value):
    high = value.astype(jnp.bfloat16)
    low = (value - high.astype(jnp.float32)).astype(jnp.bfloat16)
    return high, low


def contract_last(left, right, precision=None):
    return lax.dot_general(
        left,
        right,
        (((1,), (1,)), ((), ())),
        precision=precision,
        preferred_element_type=jnp.float32,
    )


def gram_kernel(scale, x_ref, prev_ref, energy_ref, packed_ref, centred_ref, high_ref, low_ref):
    walkers = centred_ref.shape[0]
    for sub in range(SUB):
        part = x_ref[pl.ds(sub, walkers, stride=SUB), :]
        part = part - jnp.sum(part, axis=0, keepdims=True) * (1.0 / walkers)
        lanes = slice(sub * LANES, (sub + 1) * LANES)
        centred_ref[:, lanes] = part
        high, low = split_high_low(part)
        high_ref[:, lanes] = high
        low_ref[:, lanes] = low
    blocks = walkers // BLOCK
    row = 0
    for i in range(blocks):
        mine = slice(i * BLOCK, (i + 1) * BLOCK)
        rest = slice(i * BLOCK, walkers)
        strip = contract_last(high_ref[mine, :], high_ref[rest, :])
        strip = strip + contract_last(high_ref[mine, :], low_ref[rest, :])
        strip = strip + contract_last(low_ref[mine, :], high_ref[rest, :])
        strip = strip * scale
        for j in range(blocks - i):
            packed_ref[row : row + BLOCK, :] = strip[:, j * BLOCK : (j + 1) * BLOCK]
            row += BLOCK
    along = contract_last(prev_ref[...], centred_ref[...], lax.Precision.HIGHEST) * scale
    for j in range(walkers // HALF):
        part = slice(j * HALF, (j + 1) * HALF)
        packed_ref[HALF + j : HALF + j + 1, :HALF] = along[:, part]
        packed_ref[HALF + SUB + j : HALF + SUB + j + 1, :HALF] = energy_ref[:, part]


def gram_pieces(received, prev_update, energy_row, walkers, scale):
    width = prev_update.shape[1]
    blocks = walkers // BLOCK
    pieces = blocks * (blocks + 1) // 2
    return pl.pallas_call(
        lambda *refs: gram_kernel(scale, *refs),
        in_specs=[pl.BlockSpec(memory_space=pltpu.VMEM)] * 3,
        out_specs=[pl.BlockSpec(memory_space=pltpu.VMEM)] * 2,
        out_shape=(
            pltpu.VMEM((pieces * BLOCK, LANES), jnp.float32),
            pltpu.VMEM((walkers, width), jnp.float32),
        ),
        scratch_shapes=[
            pltpu.VMEM((walkers, width), jnp.bfloat16),
            pltpu.VMEM((walkers, width), jnp.bfloat16),
        ],
        name="gram_pieces",
    )(received, prev_update, energy_row)


def near(value):
    return pltpu.with_memory_space_constraint(value, pltpu.VMEM)


def matmul(left, right, left_dim=1, right_dim=0):
    return lax.dot_general(
        left,
        right,
        (((left_dim,), (right_dim,)), ((), ())),
        precision=lax.Precision.HIGHEST,
        preferred_element_type=jnp.float32,
    )


def reduce_panel(panel, first):
    full = (SUB, BLOCK)
    lane = lax.broadcasted_iota(jnp.int32, full, 1)
    row_of = lax.broadcasted_iota(jnp.int32, full, 0)
    pivots = [jnp.broadcast_to(panel[:, first + k : first + k + 1], full) for k in range(SUB)]
    for k in range(SUB):
        column = pivots[k]
        scale = 1.0 / jnp.broadcast_to(column[k : k + 1, :], full)
        mine = row_of == k
        here = lane == first + k
        row = jnp.broadcast_to(panel[k : k + 1, :], full)
        row = jnp.where(here, scale, row * scale)
        panel = jnp.where(mine, row, jnp.where(here, 0.0, panel) - column * row)
        for j in range(k + 1, SUB):
            other = jnp.broadcast_to(pivots[j][k : k + 1, :], full) * scale
            pivots[j] = jnp.where(mine, other, pivots[j] - column * other)
    return panel


def inverse(block):
    full = (SUB, BLOCK)
    lane = lax.broadcasted_iota(jnp.int32, full, 1)
    groups = [block[i : i + SUB] for i in range(0, BLOCK, SUB)]
    for g, first in enumerate(range(0, BLOCK, SUB)):
        panel = reduce_panel(groups[g], first)
        rows = [jnp.broadcast_to(panel[k : k + 1, :], full) for k in range(SUB)]
        here = (lane >= first) & (lane < first + SUB)
        for i, value in enumerate(groups):
            if i != g:
                left = jnp.where(here, 0.0, value)
                for k in range(SUB):
                    left = left - value[:, first + k : first + k + 1] * rows[k]
                groups[i] = left
        groups[g] = panel
    return jnp.concatenate(groups, axis=0)


def solve_kernel(whole_ref, centred_ref, prev_ref, out_ref):
    lane = lax.broadcasted_iota(jnp.int32, (BLOCK, BLOCK), 1)
    row_of = lax.broadcasted_iota(jnp.int32, (BLOCK, BLOCK), 0)
    shift = jnp.where(lane == row_of, damping, 0.0)
    walkers = centred_ref.shape[0]

    def gram(index):
        return whole_ref[index * BLOCK : (index + 1) * BLOCK, :]

    def vector(first):
        halves = [whole_ref[first + j : first + j + 1, :HALF] for j in range(walkers // HALF)]
        return [jnp.concatenate(halves[j : j + 2], axis=1) for j in range(0, len(halves), 2)]

    along = vector(HALF)
    energies = vector(HALF + SUB)
    corner = whole_ref[:HALF, HALF:BLOCK].T
    lower = jnp.concatenate([corner, whole_ref[HALF:BLOCK, HALF:BLOCK]], axis=1)
    g00 = jnp.concatenate([whole_ref[:HALF, :], lower], axis=0)
    mean = sum(jnp.sum(part, axis=1, keepdims=True) for part in energies) * (1.0 / walkers)
    right = [
        (mean - energy) * (1.0 / math.sqrt(walkers)) - momentum * part
        for energy, part in zip(energies, along)
    ]
    g01, g02, g12 = gram(1), gram(2), gram(4)
    inv0 = inverse(g00 + shift)
    w01, w02 = matmul(inv0, g01), matmul(inv0, g02)
    s11 = gram(3) + shift - matmul(g01, w01, 0, 0)
    s12 = g12 - matmul(g01, w02, 0, 0)
    s22 = gram(5) + shift - matmul(g02, w02, 0, 0)
    y0 = matmul(right[0], inv0)
    r1 = right[1] - matmul(y0, g01)
    r2 = right[2] - matmul(y0, g02)
    inv1 = inverse(s11)
    w12 = matmul(inv1, s12)
    s22 = s22 - matmul(s12, w12, 0, 0)
    y1 = matmul(r1, inv1)
    r2 = r2 - matmul(y1, s12)
    inv2 = inverse(s22)
    x2 = matmul(r2, inv2)
    x1 = y1 - matmul(x2, w12, 1, 1)
    x0 = y0 - matmul(x1, w01, 1, 1) - matmul(x2, w02, 1, 1)
    out_ref[...] = (
        matmul(x0, centred_ref[0:BLOCK, :])
        + matmul(x1, centred_ref[BLOCK : 2 * BLOCK, :])
        + matmul(x2, centred_ref[2 * BLOCK :, :])
        + momentum * prev_ref[...]
    )


def solve_update(whole, centred, prev_update):
    return pl.pallas_call(
        solve_kernel,
        in_specs=[pl.BlockSpec(memory_space=pltpu.VMEM)] * 3,
        out_specs=pl.BlockSpec(memory_space=pltpu.VMEM),
        out_shape=jax.ShapeDtypeStruct(prev_update.shape, jnp.float32),
        name="solve_update",
    )(whole, centred, prev_update)


def exchange(pieces, axes):
    return lax.all_to_all(pieces, axes, split_axis=0, concat_axis=0, tiled=True)


def hand_round(value, axes):
    return exchange(jnp.broadcast_to(value[None], (lax.axis_size(axes), *value.shape)), axes)


def body(
    jacobian,
    prev_update,
    base_energy,
    elec_pos,
    atom_pos,
    quad_ratio,
    rotation,
    channels,
    ecp_coef,
    ecp_expo,
):
    owners = lax.axis_size(WALK)
    columns = lax.axis_size(COL)
    rows, width = jacobian.shape
    walkers = rows * owners
    scale = 1.0 / (width * columns)
    pieces = dense_pieces(jacobian, owners).reshape(owners, rows * SUB, LANES)
    received = exchange(pieces, WALK)
    energy_mine = base_energy + nonlocal_energy(
        elec_pos, atom_pos, quad_ratio, rotation, channels, ecp_coef, ecp_expo
    )
    energy_row = lax.dynamic_update_slice(
        jnp.zeros((1, walkers), jnp.float32),
        energy_mine[None, :] / columns,
        (0, lax.axis_index(WALK) * rows),
    )
    packed, centred = gram_pieces(
        near(received.reshape(walkers * SUB, LANES)), prev_update, near(energy_row), walkers, scale
    )
    plane = lax.axis_size(PLANE)
    share = jnp.sum(exchange(packed.reshape(plane, -1, LANES), PLANE), axis=0)
    share = jnp.sum(hand_round(share, "z"), axis=0)
    whole = hand_round(share, PLANE)
    update_mine = solve_update(near(whole.reshape(packed.shape)), near(centred), prev_update)
    return (energy_mine, update_mine)


def solution(mesh):
    mesh = jax.sharding.Mesh(mesh.devices.reshape(16, 4, 4, 2), ("z", "y", "x", "core"))
    in_specs = (
        P(WALK, COL),
        P(COL, WALK),
        P(WALK),
        P(WALK, None, None),
        P(),
        P(WALK, None, None, None),
        P(WALK, None),
        P(),
        P(),
        P(),
    )
    out_specs = (P(WALK), P(COL, WALK))
    return jax.shard_map(body, mesh=mesh, in_specs=in_specs, out_specs=out_specs, check_vma=False)
```

```python
import math

import jax
import jax.numpy as jnp
from jax import lax
from jax.experimental import pallas as pl
from jax.experimental.pallas import tpu as pltpu
from jax.sharding import PartitionSpec as P

NROT = 16


momentum = 0.9
damping = 0.1


def icosa_points():
    golden = (1.0 + math.sqrt(5.0)) / 2.0
    length = math.sqrt(1.0 + golden * golden)
    rows = []
    for first in (-1.0, 1.0):
        for second in (-golden, golden):
            rows.append((0.0, first / length, second / length))
            rows.append((first / length, second / length, 0.0))
            rows.append((second / length, 0.0, first / length))
    return jnp.asarray(rows, dtype=jnp.float32).T


def rotation_table(count):
    angle = jnp.arange(count, dtype=jnp.float32)
    turn_z = 2.0 * math.pi * angle / count
    turn_x = 0.9 * angle
    cz, sz = (jnp.cos(turn_z), jnp.sin(turn_z))
    cx, sx = (jnp.cos(turn_x), jnp.sin(turn_x))
    zeros = jnp.zeros_like(cz)
    matrix = jnp.stack(
        [
            jnp.stack([cz, -sz * cx, sz * sx], axis=-1),
            jnp.stack([sz, cz * cx, -cz * sx], axis=-1),
            jnp.stack([zeros, sx, cx], axis=-1),
        ],
        axis=1,
    )
    points = icosa_points()
    rotated = matrix[:, :, 0, None] * points[None, 0, :]
    rotated = rotated + matrix[:, :, 1, None] * points[None, 1, :]
    rotated = rotated + matrix[:, :, 2, None] * points[None, 2, :]
    return rotated.reshape(count, -1)


def nonlocal_energy(elec_pos, atom_pos, quad_ratio, rotation, channels, ecp_coef, ecp_expo):
    walkers, electrons = rotation.shape
    count = NROT
    table = rotation_table(count)
    onehot = (rotation[:, :, None] == jnp.arange(count, dtype=jnp.int32)[None, None, :]).astype(
        jnp.float32
    )
    rotated = jnp.einsum("wek,kf->wef", onehot, table, precision=lax.Precision.HIGHEST)
    rotated = rotated.reshape(walkers, electrons, 3, -1)
    diff = elec_pos[:, :, None, :] - atom_pos[None, :, :, None]
    dist2 = jnp.sum(diff * diff, axis=1)
    unit = diff / jnp.sqrt(dist2 + 0.01)[:, None, :, :]
    cosang = unit[:, 0, :, :, None] * rotated[:, None, :, 0, :]
    cosang = cosang + unit[:, 1, :, :, None] * rotated[:, None, :, 1, :]
    cosang = cosang + unit[:, 2, :, :, None] * rotated[:, None, :, 2, :]
    quad = quad_ratio.shape[-1]
    lmax = ecp_coef.shape[1]
    lower = jnp.ones_like(cosang)
    upper = cosang
    total = jnp.zeros((walkers,), jnp.float32)
    for level in range(lmax):
        if level == 0:
            poly = lower
        elif level == 1:
            poly = upper
        else:
            fresh = ((2 * level - 1) * cosang * upper - (level - 1) * lower) / level
            lower, upper = (upper, fresh)
            poly = fresh
        angular = jnp.sum(poly * quad_ratio, axis=-1) / quad
        active = (channels > level).astype(jnp.float32)
        radial = ecp_coef[None, :, level, None] * jnp.exp(-ecp_expo[None, :, level, None] * dist2)
        term = (2 * level + 1) * active[None, :, None] * radial * angular
        total = total + jnp.sum(term, axis=(1, 2))
    return total


BLOCK = 128
HALF = 64
EXTRA = 16
SUB = 8
LANES = 128
WALK = ("z", "y")
COL = ("x", "core")
PLANE = ("core", "x", "y")


def spread_rows(jac_ref, out_ref):
    rows = jac_ref.shape[0]
    for tile in range(jac_ref.shape[1] // LANES):
        owner, sub = divmod(tile, SUB)
        out_ref[pl.ds(owner * rows * SUB + sub, rows, stride=SUB), :] = jac_ref[
            :, tile * LANES : (tile + 1) * LANES
        ]


def dense_pieces(jacobian, owners):
    rows, width = jacobian.shape
    steps = 2
    piece = width // owners
    assert piece == SUB * LANES
    return pl.pallas_call(
        spread_rows,
        grid=(steps,),
        in_specs=[pl.BlockSpec((rows, width // steps), lambda i: (0, i))],
        out_specs=pl.BlockSpec((owners // steps * rows * SUB, LANES), lambda i: (i, 0)),
        out_shape=jax.ShapeDtypeStruct((owners * rows * SUB, LANES), jnp.float32),
        name="dense_pieces",
    )(jacobian)


def split_high_low(value):
    high = value.astype(jnp.bfloat16)
    low = (value - high.astype(jnp.float32)).astype(jnp.bfloat16)
    return high, low


def contract_last(left, right):
    return lax.dot_general(
        left,
        right,
        (((1,), (1,)), ((), ())),
        preferred_element_type=jnp.float32,
    )


def gram_kernel(scale, x_ref, prev_ref, energy_ref, packed_ref, centred_ref):
    walkers = centred_ref.shape[0]
    blocks = walkers // BLOCK
    prev_parts = split_high_low(prev_ref[...])
    strips = [None] * blocks
    for sub in range(0, SUB, 2):
        parts = []
        for s in (sub, sub + 1):
            part = x_ref[pl.ds(s, walkers, stride=SUB), :]
            part = part - jnp.sum(part, axis=0, keepdims=True) * (1.0 / walkers)
            centred_ref[:, s * LANES : (s + 1) * LANES] = part
            parts.append(part)
        high, low = split_high_low(jnp.concatenate(parts, axis=1))
        lanes = slice(sub * LANES, (sub + 2) * LANES)
        for i in range(blocks):
            left = [part[i * BLOCK : (i + 1) * BLOCK] for part in (high, low)]
            if i == 0:
                extra = [jnp.broadcast_to(p[:, lanes], (EXTRA, 2 * LANES)) for p in prev_parts]
                left = [jnp.concatenate(pair, axis=0) for pair in zip(left, extra)]
            strip = contract_last(left[0], high[i * BLOCK :])
            strip = strip + contract_last(left[0], low[i * BLOCK :])
            strip = strip + contract_last(left[1], high[i * BLOCK :])
            strips[i] = strip if strips[i] is None else strips[i] + strip
    row = 0
    for i in range(blocks):
        strip = strips[i] * scale
        for j in range(blocks - i):
            packed_ref[row : row + BLOCK, :] = strip[:BLOCK, j * BLOCK : (j + 1) * BLOCK]
            row += BLOCK
    along = strips[0][BLOCK : BLOCK + 1, :] * scale
    for j in range(walkers // HALF):
        part = slice(j * HALF, (j + 1) * HALF)
        packed_ref[HALF + j : HALF + j + 1, :HALF] = along[:, part]
        packed_ref[HALF + SUB + j : HALF + SUB + j + 1, :HALF] = energy_ref[:, part]


def gram_pieces(received, prev_update, energy_row, walkers, scale):
    width = prev_update.shape[1]
    blocks = walkers // BLOCK
    pieces = blocks * (blocks + 1) // 2
    return pl.pallas_call(
        lambda *refs: gram_kernel(scale, *refs),
        in_specs=[pl.BlockSpec(memory_space=pltpu.VMEM)] * 3,
        out_specs=[pl.BlockSpec(memory_space=pltpu.VMEM)] * 2,
        out_shape=(
            pltpu.VMEM((pieces * BLOCK, LANES), jnp.float32),
            pltpu.VMEM((walkers, width), jnp.float32),
        ),
        name="gram_pieces",
    )(received, prev_update, energy_row)


def near(value):
    return pltpu.with_memory_space_constraint(value, pltpu.VMEM)


def matmul(left, right, left_dim=1, right_dim=0):
    return lax.dot_general(
        left,
        right,
        (((left_dim,), (right_dim,)), ((), ())),
        precision=lax.Precision.HIGHEST,
        preferred_element_type=jnp.float32,
    )


def reduce_panel(panel, first):
    full = (SUB, BLOCK)
    lane = lax.broadcasted_iota(jnp.int32, full, 1)
    row_of = lax.broadcasted_iota(jnp.int32, full, 0)
    pivots = [jnp.broadcast_to(panel[:, first + k : first + k + 1], full) for k in range(SUB)]
    for k in range(SUB):
        column = pivots[k]
        scale = 1.0 / jnp.broadcast_to(column[k : k + 1, :], full)
        mine = row_of == k
        here = lane == first + k
        row = jnp.broadcast_to(panel[k : k + 1, :], full)
        row = jnp.where(here, scale, row * scale)
        panel = jnp.where(mine, row, jnp.where(here, 0.0, panel) - column * row)
        for j in range(k + 1, SUB):
            other = jnp.broadcast_to(pivots[j][k : k + 1, :], full) * scale
            pivots[j] = jnp.where(mine, other, pivots[j] - column * other)
    return panel


def inverse(block):
    full = (SUB, BLOCK)
    lane = lax.broadcasted_iota(jnp.int32, full, 1)
    groups = [block[i : i + SUB] for i in range(0, BLOCK, SUB)]
    for g, first in enumerate(range(0, BLOCK, SUB)):
        panel = reduce_panel(groups[g], first)
        rows = [jnp.broadcast_to(panel[k : k + 1, :], full) for k in range(SUB)]
        here = (lane >= first) & (lane < first + SUB)
        for i in [*range(g + 1, len(groups)), *range(g)]:
            left = jnp.where(here, 0.0, groups[i])
            for k in range(SUB):
                left = left - groups[i][:, first + k : first + k + 1] * rows[k]
            groups[i] = left
        groups[g] = panel
    return jnp.concatenate(groups, axis=0)


def solve_kernel(whole_ref, centred_ref, prev_ref, out_ref):
    lane = lax.broadcasted_iota(jnp.int32, (BLOCK, BLOCK), 1)
    row_of = lax.broadcasted_iota(jnp.int32, (BLOCK, BLOCK), 0)
    shift = jnp.where(lane == row_of, damping, 0.0)
    walkers = centred_ref.shape[0]

    def gram(index):
        return whole_ref[index * BLOCK : (index + 1) * BLOCK, :]

    def vector(first):
        halves = [whole_ref[first + j : first + j + 1, :HALF] for j in range(walkers // HALF)]
        return [jnp.concatenate(halves[j : j + 2], axis=1) for j in range(0, len(halves), 2)]

    along = vector(HALF)
    energies = vector(HALF + SUB)
    corner = whole_ref[:HALF, HALF:BLOCK].T
    lower = jnp.concatenate([corner, whole_ref[HALF:BLOCK, HALF:BLOCK]], axis=1)
    g00 = jnp.concatenate([whole_ref[:HALF, :], lower], axis=0)
    mean = sum(jnp.sum(part, axis=1, keepdims=True) for part in energies) * (1.0 / walkers)
    right = [
        (mean - energy) * (1.0 / math.sqrt(walkers)) - momentum * part
        for energy, part in zip(energies, along)
    ]
    g01, g02, g12 = gram(1), gram(2), gram(4)
    inv0 = inverse(g00 + shift)
    w01, w02 = matmul(inv0, g01), matmul(inv0, g02)
    s11 = gram(3) + shift - matmul(g01, w01, 0, 0)
    s12 = g12 - matmul(g01, w02, 0, 0)
    s22 = gram(5) + shift - matmul(g02, w02, 0, 0)
    y0 = matmul(right[0], inv0)
    r1 = right[1] - matmul(y0, g01)
    r2 = right[2] - matmul(y0, g02)
    inv1 = inverse(s11)
    w12 = matmul(inv1, s12)
    s22 = s22 - matmul(s12, w12, 0, 0)
    y1 = matmul(r1, inv1)
    r2 = r2 - matmul(y1, s12)
    y0 = y0 - matmul(y1, w01, 1, 1)
    w02 = w02 - matmul(w01, w12)
    inv2 = inverse(s22)
    x2 = matmul(r2, inv2)
    x1 = y1 - matmul(x2, w12, 1, 1)
    x0 = y0 - matmul(x2, w02, 1, 1)
    total = jnp.zeros((SUB, out_ref.shape[1]), jnp.float32)
    for i, solved in enumerate((x0, x1, x2)):
        solved = jnp.broadcast_to(solved, (BLOCK, BLOCK))
        column = jnp.sum(jnp.where(lane == row_of, solved, 0.0), axis=1, keepdims=True)
        terms = centred_ref[i * BLOCK : (i + 1) * BLOCK, :] * column
        total = total + jnp.sum(terms.reshape(BLOCK // SUB, SUB, -1), axis=0)
    out_ref[...] = jnp.sum(total, axis=0, keepdims=True) + momentum * prev_ref[...]


def solve_update(whole, centred, prev_update):
    return pl.pallas_call(
        solve_kernel,
        in_specs=[pl.BlockSpec(memory_space=pltpu.VMEM)] * 3,
        out_specs=pl.BlockSpec(memory_space=pltpu.VMEM),
        out_shape=jax.ShapeDtypeStruct(prev_update.shape, jnp.float32),
        name="solve_update",
    )(whole, centred, prev_update)


def exchange(pieces, axes):
    return lax.all_to_all(pieces, axes, split_axis=0, concat_axis=0, tiled=True)


def hand_round(value, axes):
    return exchange(jnp.broadcast_to(value[None], (lax.axis_size(axes), *value.shape)), axes)


def body(
    jacobian,
    prev_update,
    base_energy,
    elec_pos,
    atom_pos,
    quad_ratio,
    rotation,
    channels,
    ecp_coef,
    ecp_expo,
):
    owners = lax.axis_size(WALK)
    columns = lax.axis_size(COL)
    rows, width = jacobian.shape
    walkers = rows * owners
    scale = 1.0 / (width * columns)
    pieces = dense_pieces(jacobian, owners).reshape(owners, rows * SUB, LANES)
    received = exchange(pieces, WALK)
    energy_mine = base_energy + nonlocal_energy(
        elec_pos, atom_pos, quad_ratio, rotation, channels, ecp_coef, ecp_expo
    )
    energy_row = lax.dynamic_update_slice(
        jnp.zeros((1, walkers), jnp.float32),
        energy_mine[None, :] / columns,
        (0, lax.axis_index(WALK) * rows),
    )
    packed, centred = gram_pieces(
        near(received.reshape(walkers * SUB, LANES)), prev_update, near(energy_row), walkers, scale
    )
    plane = lax.axis_size(PLANE)
    share = jnp.sum(exchange(packed.reshape(plane, -1, LANES), PLANE), axis=0)
    share = jnp.sum(hand_round(share, "z"), axis=0)
    whole = hand_round(share, PLANE)
    update_mine = solve_update(near(whole.reshape(packed.shape)), near(centred), prev_update)
    return (energy_mine, update_mine)


def solution(mesh):
    mesh = jax.sharding.Mesh(mesh.devices.reshape(16, 4, 4, 2), ("z", "y", "x", "core"))
    in_specs = (
        P(WALK, COL),
        P(COL, WALK),
        P(WALK),
        P(WALK, None, None),
        P(),
        P(WALK, None, None, None),
        P(WALK, None),
        P(),
        P(),
        P(),
    )
    out_specs = (P(WALK), P(COL, WALK))
    return jax.shard_map(body, mesh=mesh, in_specs=in_specs, out_specs=out_specs, check_vma=False)
```

```python
import math

import jax
import jax.numpy as jnp
from jax import lax
from jax.experimental import pallas as pl
from jax.experimental.pallas import tpu as pltpu
from jax.sharding import PartitionSpec as P

NROT = 16


momentum = 0.9
damping = 0.1


def icosa_points():
    golden = (1.0 + math.sqrt(5.0)) / 2.0
    length = math.sqrt(1.0 + golden * golden)
    rows = []
    for first in (-1.0, 1.0):
        for second in (-golden, golden):
            rows.append((0.0, first / length, second / length))
            rows.append((first / length, second / length, 0.0))
            rows.append((second / length, 0.0, first / length))
    return jnp.asarray(rows, dtype=jnp.float32).T


def rotation_table(count):
    angle = jnp.arange(count, dtype=jnp.float32)
    turn_z = 2.0 * math.pi * angle / count
    turn_x = 0.9 * angle
    cz, sz = (jnp.cos(turn_z), jnp.sin(turn_z))
    cx, sx = (jnp.cos(turn_x), jnp.sin(turn_x))
    zeros = jnp.zeros_like(cz)
    matrix = jnp.stack(
        [
            jnp.stack([cz, -sz * cx, sz * sx], axis=-1),
            jnp.stack([sz, cz * cx, -cz * sx], axis=-1),
            jnp.stack([zeros, sx, cx], axis=-1),
        ],
        axis=1,
    )
    points = icosa_points()
    rotated = matrix[:, :, 0, None] * points[None, 0, :]
    rotated = rotated + matrix[:, :, 1, None] * points[None, 1, :]
    rotated = rotated + matrix[:, :, 2, None] * points[None, 2, :]
    return rotated.reshape(count, -1)


def nonlocal_energy(elec_pos, atom_pos, quad_ratio, rotation, channels, ecp_coef, ecp_expo):
    walkers, electrons = rotation.shape
    count = NROT
    table = rotation_table(count)
    onehot = (rotation[:, :, None] == jnp.arange(count, dtype=jnp.int32)[None, None, :]).astype(
        jnp.float32
    )
    rotated = jnp.einsum("wek,kf->wef", onehot, table, precision=lax.Precision.HIGHEST)
    rotated = rotated.reshape(walkers, electrons, 3, -1)
    diff = elec_pos[:, :, None, :] - atom_pos[None, :, :, None]
    dist2 = jnp.sum(diff * diff, axis=1)
    unit = diff / jnp.sqrt(dist2 + 0.01)[:, None, :, :]
    cosang = unit[:, 0, :, :, None] * rotated[:, None, :, 0, :]
    cosang = cosang + unit[:, 1, :, :, None] * rotated[:, None, :, 1, :]
    cosang = cosang + unit[:, 2, :, :, None] * rotated[:, None, :, 2, :]
    quad = quad_ratio.shape[-1]
    lmax = ecp_coef.shape[1]
    lower = jnp.ones_like(cosang)
    upper = cosang
    total = jnp.zeros((walkers,), jnp.float32)
    for level in range(lmax):
        if level == 0:
            poly = lower
        elif level == 1:
            poly = upper
        else:
            fresh = ((2 * level - 1) * cosang * upper - (level - 1) * lower) / level
            lower, upper = (upper, fresh)
            poly = fresh
        angular = jnp.sum(poly * quad_ratio, axis=-1) / quad
        active = (channels > level).astype(jnp.float32)
        radial = ecp_coef[None, :, level, None] * jnp.exp(-ecp_expo[None, :, level, None] * dist2)
        term = (2 * level + 1) * active[None, :, None] * radial * angular
        total = total + jnp.sum(term, axis=(1, 2))
    return total


BLOCK = 128
HALF = 64
EXTRA = 16
SUB = 8
LANES = 128
WALK = ("z", "y")
COL = ("x", "core")
PLANE = ("core", "x", "y")


def spread_rows(jac_ref, out_ref, buffer_ref, sems):
    rows, width = jac_ref.shape
    chunks = sems.shape[0]
    part = width // chunks
    copies = []
    for c in range(chunks):
        lanes = slice(c * part, (c + 1) * part)
        copy = pltpu.make_async_copy(jac_ref.at[:, lanes], buffer_ref.at[:, lanes], sems.at[c])
        copy.start()
        copies.append(copy)
    for c in range(chunks):
        copies[c].wait()
        for tile in range(c * part // LANES, (c + 1) * part // LANES):
            owner, sub = divmod(tile, SUB)
            out_ref[pl.ds(owner * rows * SUB + sub, rows, stride=SUB), :] = buffer_ref[
                :, tile * LANES : (tile + 1) * LANES
            ]


def dense_pieces(jacobian, owners):
    rows, width = jacobian.shape
    chunks = 8
    assert width // owners == SUB * LANES
    return pl.pallas_call(
        spread_rows,
        in_specs=[pl.BlockSpec(memory_space=pl.ANY)],
        out_specs=pl.BlockSpec(memory_space=pltpu.VMEM),
        out_shape=pltpu.VMEM((owners * rows * SUB, LANES), jnp.float32),
        scratch_shapes=[
            pltpu.VMEM((rows, width), jnp.float32),
            pltpu.SemaphoreType.DMA((chunks,)),
        ],
        name="dense_pieces",
    )(jacobian)


def split_high_low(value):
    high = value.astype(jnp.bfloat16)
    low = (value - high.astype(jnp.float32)).astype(jnp.bfloat16)
    return high, low


def contract_last(left, right):
    return lax.dot_general(
        left,
        right,
        (((1,), (1,)), ((), ())),
        preferred_element_type=jnp.float32,
    )


def gram_kernel(scale, x_ref, prev_ref, energy_ref, packed_ref, centred_ref):
    walkers = centred_ref.shape[0]
    blocks = walkers // BLOCK
    prev_parts = split_high_low(prev_ref[...])
    strips = [None] * blocks
    for sub in range(0, SUB, 2):
        parts = []
        for s in (sub, sub + 1):
            part = x_ref[pl.ds(s, walkers, stride=SUB), :]
            part = part - jnp.sum(part, axis=0, keepdims=True) * (1.0 / walkers)
            centred_ref[:, s * LANES : (s + 1) * LANES] = part
            parts.append(part)
        high, low = split_high_low(jnp.concatenate(parts, axis=1))
        lanes = slice(sub * LANES, (sub + 2) * LANES)
        for i in range(blocks):
            left = [part[i * BLOCK : (i + 1) * BLOCK] for part in (high, low)]
            if i == 0:
                extra = [jnp.broadcast_to(p[:, lanes], (EXTRA, 2 * LANES)) for p in prev_parts]
                left = [jnp.concatenate(pair, axis=0) for pair in zip(left, extra)]
            strip = contract_last(left[0], high[i * BLOCK :])
            strip = strip + contract_last(left[0], low[i * BLOCK :])
            strip = strip + contract_last(left[1], high[i * BLOCK :])
            strips[i] = strip if strips[i] is None else strips[i] + strip
    row = 0
    for i in range(blocks):
        strip = strips[i] * scale
        for j in range(blocks - i):
            packed_ref[row : row + BLOCK, :] = strip[:BLOCK, j * BLOCK : (j + 1) * BLOCK]
            row += BLOCK
    along = strips[0][BLOCK : BLOCK + 1, :] * scale
    for j in range(walkers // HALF):
        part = slice(j * HALF, (j + 1) * HALF)
        packed_ref[HALF + j : HALF + j + 1, :HALF] = along[:, part]
        packed_ref[HALF + SUB + j : HALF + SUB + j + 1, :HALF] = energy_ref[:, part]


def gram_pieces(received, prev_update, energy_row, walkers, scale):
    width = prev_update.shape[1]
    blocks = walkers // BLOCK
    pieces = blocks * (blocks + 1) // 2
    return pl.pallas_call(
        lambda *refs: gram_kernel(scale, *refs),
        in_specs=[pl.BlockSpec(memory_space=pltpu.VMEM)] * 3,
        out_specs=[pl.BlockSpec(memory_space=pltpu.VMEM)] * 2,
        out_shape=(
            pltpu.VMEM((pieces * BLOCK, LANES), jnp.float32),
            pltpu.VMEM((walkers, width), jnp.float32),
        ),
        name="gram_pieces",
    )(received, prev_update, energy_row)


def near(value):
    return pltpu.with_memory_space_constraint(value, pltpu.VMEM)


def split_three(value):
    high, low = split_high_low(value)
    rest = value - high.astype(jnp.float32)
    return high, low, (rest - low.astype(jnp.float32)).astype(jnp.bfloat16)


def matmul(left, right, left_dim=1, right_dim=0):
    lh, lm, ll = split_three(left)
    rh, rm, rl = split_three(right)
    return lax.dot_general(
        jnp.concatenate([lh, lh, lm, lm, lh, ll], axis=left_dim),
        jnp.concatenate([rh, rm, rh, rm, rl, rh], axis=right_dim),
        (((left_dim,), (right_dim,)), ((), ())),
        preferred_element_type=jnp.float32,
    )


def reduce_panel(panel, first):
    full = (SUB, BLOCK)
    lane = lax.broadcasted_iota(jnp.int32, full, 1)
    row_of = lax.broadcasted_iota(jnp.int32, full, 0)
    pivots = [jnp.broadcast_to(panel[:, first + k : first + k + 1], full) for k in range(SUB)]
    for k in range(SUB):
        column = pivots[k]
        scale = 1.0 / jnp.broadcast_to(column[k : k + 1, :], full)
        mine = row_of == k
        here = lane == first + k
        row = jnp.broadcast_to(panel[k : k + 1, :], full)
        row = jnp.where(here, scale, row * scale)
        panel = jnp.where(mine, row, jnp.where(here, 0.0, panel) - column * row)
        for j in range(k + 1, SUB):
            other = jnp.broadcast_to(pivots[j][k : k + 1, :], full) * scale
            pivots[j] = jnp.where(mine, other, pivots[j] - column * other)
    return panel


def inverse(block):
    full = (SUB, BLOCK)
    lane = lax.broadcasted_iota(jnp.int32, full, 1)
    groups = [block[i : i + SUB] for i in range(0, BLOCK, SUB)]
    for g, first in enumerate(range(0, BLOCK, SUB)):
        panel = reduce_panel(groups[g], first)
        rows = [jnp.broadcast_to(panel[k : k + 1, :], full) for k in range(SUB)]
        here = (lane >= first) & (lane < first + SUB)
        for i in [*range(g + 1, len(groups)), *range(g)]:
            left = jnp.where(here, 0.0, groups[i])
            for k in range(SUB):
                left = left - groups[i][:, first + k : first + k + 1] * rows[k]
            groups[i] = left
        groups[g] = panel
    return jnp.concatenate(groups, axis=0)


def solve_kernel(whole_ref, centred_ref, prev_ref, out_ref):
    lane = lax.broadcasted_iota(jnp.int32, (BLOCK, BLOCK), 1)
    row_of = lax.broadcasted_iota(jnp.int32, (BLOCK, BLOCK), 0)
    shift = jnp.where(lane == row_of, damping, 0.0)
    walkers = centred_ref.shape[0]

    def gram(index):
        return whole_ref[index * BLOCK : (index + 1) * BLOCK, :]

    def vector(first):
        halves = [whole_ref[first + j : first + j + 1, :HALF] for j in range(walkers // HALF)]
        return [jnp.concatenate(halves[j : j + 2], axis=1) for j in range(0, len(halves), 2)]

    along = vector(HALF)
    energies = vector(HALF + SUB)
    corner = whole_ref[:HALF, HALF:BLOCK].T
    lower = jnp.concatenate([corner, whole_ref[HALF:BLOCK, HALF:BLOCK]], axis=1)
    g00 = jnp.concatenate([whole_ref[:HALF, :], lower], axis=0)
    mean = sum(jnp.sum(part, axis=1, keepdims=True) for part in energies) * (1.0 / walkers)
    right = [
        (mean - energy) * (1.0 / math.sqrt(walkers)) - momentum * part
        for energy, part in zip(energies, along)
    ]
    g01, g02, g12 = gram(1), gram(2), gram(4)
    inv0 = inverse(g00 + shift)
    w01, w02 = matmul(inv0, g01), matmul(inv0, g02)
    s11 = gram(3) + shift - matmul(g01, w01, 0, 0)
    s12 = g12 - matmul(g01, w02, 0, 0)
    s22 = gram(5) + shift - matmul(g02, w02, 0, 0)
    y0 = matmul(right[0], inv0)
    r1 = right[1] - matmul(y0, g01)
    r2 = right[2] - matmul(y0, g02)
    inv1 = inverse(s11)
    w12 = matmul(inv1, s12)
    s22 = s22 - matmul(s12, w12, 0, 0)
    y1 = matmul(r1, inv1)
    r2 = r2 - matmul(y1, s12)
    y0 = y0 - matmul(y1, w01, 1, 1)
    w02 = w02 - matmul(w01, w12)
    inv2 = inverse(s22)
    x2 = matmul(r2, inv2)
    x1 = y1 - matmul(x2, w12, 1, 1)
    x0 = y0 - matmul(x2, w02, 1, 1)
    total = jnp.zeros((SUB, out_ref.shape[1]), jnp.float32)
    for i, solved in enumerate((x0, x1, x2)):
        solved = jnp.broadcast_to(solved, (BLOCK, BLOCK))
        column = jnp.sum(jnp.where(lane == row_of, solved, 0.0), axis=1, keepdims=True)
        terms = centred_ref[i * BLOCK : (i + 1) * BLOCK, :] * column
        total = total + jnp.sum(terms.reshape(BLOCK // SUB, SUB, -1), axis=0)
    out_ref[...] = jnp.sum(total, axis=0, keepdims=True) + momentum * prev_ref[...]


def solve_update(whole, centred, prev_update):
    return pl.pallas_call(
        solve_kernel,
        in_specs=[pl.BlockSpec(memory_space=pltpu.VMEM)] * 3,
        out_specs=pl.BlockSpec(memory_space=pltpu.VMEM),
        out_shape=jax.ShapeDtypeStruct(prev_update.shape, jnp.float32),
        name="solve_update",
    )(whole, centred, prev_update)


def exchange(pieces, axes):
    return lax.all_to_all(pieces, axes, split_axis=0, concat_axis=0, tiled=True)


def hand_round(value, axes):
    return exchange(jnp.broadcast_to(value[None], (lax.axis_size(axes), *value.shape)), axes)


def body(
    jacobian,
    prev_update,
    base_energy,
    elec_pos,
    atom_pos,
    quad_ratio,
    rotation,
    channels,
    ecp_coef,
    ecp_expo,
):
    owners = lax.axis_size(WALK)
    columns = lax.axis_size(COL)
    rows, width = jacobian.shape
    walkers = rows * owners
    scale = 1.0 / (width * columns)
    pieces = dense_pieces(jacobian, owners).reshape(owners, rows * SUB, LANES)
    received = exchange(pieces, WALK)
    energy_mine = base_energy + nonlocal_energy(
        elec_pos, atom_pos, quad_ratio, rotation, channels, ecp_coef, ecp_expo
    )
    energy_row = lax.dynamic_update_slice(
        jnp.zeros((1, walkers), jnp.float32),
        energy_mine[None, :] / columns,
        (0, lax.axis_index(WALK) * rows),
    )
    packed, centred = gram_pieces(
        near(received.reshape(walkers * SUB, LANES)), prev_update, near(energy_row), walkers, scale
    )
    plane = lax.axis_size(PLANE)
    share = jnp.sum(exchange(packed.reshape(plane, -1, LANES), PLANE), axis=0)
    share = jnp.sum(hand_round(share, "z"), axis=0)
    whole = hand_round(share, PLANE)
    update_mine = solve_update(near(whole.reshape(packed.shape)), near(centred), prev_update)
    return (energy_mine, update_mine)


def solution(mesh):
    mesh = jax.sharding.Mesh(mesh.devices.reshape(16, 4, 4, 2), ("z", "y", "x", "core"))
    in_specs = (
        P(WALK, COL),
        P(COL, WALK),
        P(WALK),
        P(WALK, None, None),
        P(),
        P(WALK, None, None, None),
        P(WALK, None),
        P(),
        P(),
        P(),
    )
    out_specs = (P(WALK), P(COL, WALK))
    return jax.shard_map(body, mesh=mesh, in_specs=in_specs, out_specs=out_specs, check_vma=False)
```

```python
import math

import jax
import jax.numpy as jnp
from jax import lax
from jax.experimental import pallas as pl
from jax.experimental.pallas import tpu as pltpu
from jax.sharding import PartitionSpec as P

NROT = 16


momentum = 0.9
damping = 0.1


def icosa_points():
    golden = (1.0 + math.sqrt(5.0)) / 2.0
    length = math.sqrt(1.0 + golden * golden)
    rows = []
    for first in (-1.0, 1.0):
        for second in (-golden, golden):
            rows.append((0.0, first / length, second / length))
            rows.append((first / length, second / length, 0.0))
            rows.append((second / length, 0.0, first / length))
    return jnp.asarray(rows, dtype=jnp.float32).T


def rotation_table(count):
    angle = jnp.arange(count, dtype=jnp.float32)
    turn_z = 2.0 * math.pi * angle / count
    turn_x = 0.9 * angle
    cz, sz = (jnp.cos(turn_z), jnp.sin(turn_z))
    cx, sx = (jnp.cos(turn_x), jnp.sin(turn_x))
    zeros = jnp.zeros_like(cz)
    matrix = jnp.stack(
        [
            jnp.stack([cz, -sz * cx, sz * sx], axis=-1),
            jnp.stack([sz, cz * cx, -cz * sx], axis=-1),
            jnp.stack([zeros, sx, cx], axis=-1),
        ],
        axis=1,
    )
    points = icosa_points()
    rotated = matrix[:, :, 0, None] * points[None, 0, :]
    rotated = rotated + matrix[:, :, 1, None] * points[None, 1, :]
    rotated = rotated + matrix[:, :, 2, None] * points[None, 2, :]
    return rotated.reshape(count, -1)


def nonlocal_energy(elec_pos, atom_pos, quad_ratio, rotation, channels, ecp_coef, ecp_expo):
    walkers, electrons = rotation.shape
    count = NROT
    table = rotation_table(count)
    onehot = (rotation[:, :, None] == jnp.arange(count, dtype=jnp.int32)[None, None, :]).astype(
        jnp.float32
    )
    rotated = jnp.einsum("wek,kf->wef", onehot, table, precision=lax.Precision.HIGHEST)
    rotated = rotated.reshape(walkers, electrons, 3, -1)
    diff = elec_pos[:, :, None, :] - atom_pos[None, :, :, None]
    dist2 = jnp.sum(diff * diff, axis=1)
    unit = diff / jnp.sqrt(dist2 + 0.01)[:, None, :, :]
    cosang = unit[:, 0, :, :, None] * rotated[:, None, :, 0, :]
    cosang = cosang + unit[:, 1, :, :, None] * rotated[:, None, :, 1, :]
    cosang = cosang + unit[:, 2, :, :, None] * rotated[:, None, :, 2, :]
    quad = quad_ratio.shape[-1]
    lmax = ecp_coef.shape[1]
    lower = jnp.ones_like(cosang)
    upper = cosang
    total = jnp.zeros((walkers,), jnp.float32)
    for level in range(lmax):
        if level == 0:
            poly = lower
        elif level == 1:
            poly = upper
        else:
            fresh = ((2 * level - 1) * cosang * upper - (level - 1) * lower) / level
            lower, upper = (upper, fresh)
            poly = fresh
        angular = jnp.sum(poly * quad_ratio, axis=-1) / quad
        active = (channels > level).astype(jnp.float32)
        radial = ecp_coef[None, :, level, None] * jnp.exp(-ecp_expo[None, :, level, None] * dist2)
        term = (2 * level + 1) * active[None, :, None] * radial * angular
        total = total + jnp.sum(term, axis=(1, 2))
    return total


BLOCK = 128
HALF = 64
EXTRA = 16
SUB = 8
LANES = 128
WALK = ("z", "y")
COL = ("x", "core")
PLANE = ("y", "core", "x")


def spread_rows(jac_ref, out_ref, taken_ref, spread_ref, in_sems, out_sems):
    rows, width = jac_ref.shape
    chunks = in_sems.shape[0]
    lanes, height = width // chunks, out_ref.shape[0] // chunks
    copies_in, copies_out = [], []
    for c in range(chunks):
        part = slice(c * lanes, (c + 1) * lanes)
        copies_in.append(
            pltpu.make_async_copy(jac_ref.at[:, part], taken_ref.at[:, part], in_sems.at[c])
        )
        part = slice(c * height, (c + 1) * height)
        copies_out.append(
            pltpu.make_async_copy(spread_ref.at[part], out_ref.at[part], out_sems.at[c])
        )
    for copy in copies_in:
        copy.start()
    for c in range(chunks):
        copies_in[c].wait()
        for tile in range(c * lanes // LANES, (c + 1) * lanes // LANES):
            owner, sub = divmod(tile, SUB)
            spread_ref[pl.ds(owner * rows * SUB + sub, rows, stride=SUB), :] = taken_ref[
                :, tile * LANES : (tile + 1) * LANES
            ]
        copies_out[c].start()
    for copy in copies_out:
        copy.wait()


def dense_pieces(jacobian, owners):
    rows, width = jacobian.shape
    chunks = 8
    assert width // owners == SUB * LANES
    shape = (owners * rows * SUB, LANES)
    return pl.pallas_call(
        spread_rows,
        in_specs=[pl.BlockSpec(memory_space=pl.ANY)],
        out_specs=pl.BlockSpec(memory_space=pl.ANY),
        out_shape=jax.ShapeDtypeStruct(shape, jnp.float32),
        scratch_shapes=[
            pltpu.VMEM((rows, width), jnp.float32),
            pltpu.VMEM(shape, jnp.float32),
            pltpu.SemaphoreType.DMA((chunks,)),
            pltpu.SemaphoreType.DMA((chunks,)),
        ],
        name="dense_pieces",
    )(jacobian)


def split_high_low(value):
    high = value.astype(jnp.bfloat16)
    low = (value - high.astype(jnp.float32)).astype(jnp.bfloat16)
    return high, low


def contract_last(left, right):
    return lax.dot_general(
        left,
        right,
        (((1,), (1,)), ((), ())),
        preferred_element_type=jnp.float32,
    )


def gram_kernel(scale, x_ref, prev_ref, energy_ref, packed_ref, centred_ref):
    walkers = centred_ref.shape[0]
    blocks = walkers // BLOCK
    prev_parts = split_high_low(prev_ref[...])
    strips = [None] * blocks
    for sub in range(0, SUB, 2):
        parts = []
        for s in (sub, sub + 1):
            part = x_ref[pl.ds(s, walkers, stride=SUB), :]
            part = part - jnp.sum(part, axis=0, keepdims=True) * (1.0 / walkers)
            centred_ref[:, s * LANES : (s + 1) * LANES] = part
            parts.append(part)
        high, low = split_high_low(jnp.concatenate(parts, axis=1))
        lanes = slice(sub * LANES, (sub + 2) * LANES)
        for i in range(blocks):
            left = [part[i * BLOCK : (i + 1) * BLOCK] for part in (high, low)]
            if i == 0:
                extra = [jnp.broadcast_to(p[:, lanes], (EXTRA, 2 * LANES)) for p in prev_parts]
                left = [jnp.concatenate(pair, axis=0) for pair in zip(left, extra)]
            strip = contract_last(left[0], high[i * BLOCK :])
            strip = strip + contract_last(left[0], low[i * BLOCK :])
            strip = strip + contract_last(left[1], high[i * BLOCK :])
            strips[i] = strip if strips[i] is None else strips[i] + strip
    row = 0
    for i in range(blocks):
        strip = strips[i] * scale
        for j in range(blocks - i):
            packed_ref[row : row + BLOCK, :] = strip[:BLOCK, j * BLOCK : (j + 1) * BLOCK]
            row += BLOCK
    along = strips[0][BLOCK : BLOCK + 1, :] * scale
    for j in range(walkers // HALF):
        part = slice(j * HALF, (j + 1) * HALF)
        packed_ref[HALF + j : HALF + j + 1, :HALF] = along[:, part]
        packed_ref[HALF + SUB + j : HALF + SUB + j + 1, :HALF] = energy_ref[:, part]


def gram_pieces(received, prev_update, energy_row, walkers, scale):
    width = prev_update.shape[1]
    blocks = walkers // BLOCK
    pieces = blocks * (blocks + 1) // 2
    return pl.pallas_call(
        lambda *refs: gram_kernel(scale, *refs),
        in_specs=[pl.BlockSpec(memory_space=pltpu.VMEM)] * 3,
        out_specs=[pl.BlockSpec(memory_space=pltpu.VMEM)] * 2,
        out_shape=(
            pltpu.VMEM((pieces * BLOCK, LANES), jnp.float32),
            pltpu.VMEM((walkers, width), jnp.float32),
        ),
        name="gram_pieces",
    )(received, prev_update, energy_row)


def near(value):
    return pltpu.with_memory_space_constraint(value, pltpu.VMEM)


def split_three(value):
    high, low = split_high_low(value)
    rest = value - high.astype(jnp.float32)
    return high, low, (rest - low.astype(jnp.float32)).astype(jnp.bfloat16)


def matmul(left, right, left_dim=1, right_dim=0):
    lh, lm, ll = split_three(left)
    rh, rm, rl = split_three(right)
    return lax.dot_general(
        jnp.concatenate([lh, lh, lm, lm, lh, ll], axis=left_dim),
        jnp.concatenate([rh, rm, rh, rm, rl, rh], axis=right_dim),
        (((left_dim,), (right_dim,)), ((), ())),
        preferred_element_type=jnp.float32,
    )


def reduce_panel(panel, first):
    full = (SUB, BLOCK)
    lane = lax.broadcasted_iota(jnp.int32, full, 1)
    row_of = lax.broadcasted_iota(jnp.int32, full, 0)
    pivots = [jnp.broadcast_to(panel[:, first + k : first + k + 1], full) for k in range(SUB)]
    for k in range(SUB):
        column = pivots[k]
        scale = 1.0 / jnp.broadcast_to(column[k : k + 1, :], full)
        mine = row_of == k
        here = lane == first + k
        row = jnp.broadcast_to(panel[k : k + 1, :], full)
        row = jnp.where(here, scale, row * scale)
        panel = jnp.where(mine, row, jnp.where(here, 0.0, panel) - column * row)
        for j in range(k + 1, SUB):
            other = jnp.broadcast_to(pivots[j][k : k + 1, :], full) * scale
            pivots[j] = jnp.where(mine, other, pivots[j] - column * other)
    return panel


def inverse(block):
    full = (SUB, BLOCK)
    lane = lax.broadcasted_iota(jnp.int32, full, 1)
    groups = [block[i : i + SUB] for i in range(0, BLOCK, SUB)]
    for g, first in enumerate(range(0, BLOCK, SUB)):
        panel = reduce_panel(groups[g], first)
        rows = [jnp.broadcast_to(panel[k : k + 1, :], full) for k in range(SUB)]
        here = (lane >= first) & (lane < first + SUB)
        for i in [*range(g + 1, len(groups)), *range(g)]:
            left = jnp.where(here, 0.0, groups[i])
            for k in range(SUB):
                left = left - groups[i][:, first + k : first + k + 1] * rows[k]
            groups[i] = left
        groups[g] = panel
    return jnp.concatenate(groups, axis=0)


def row_sums(block, row):
    return jnp.sum(block * row, axis=1, keepdims=True)


def solve_kernel(whole_ref, centred_ref, prev_ref, out_ref):
    lane = lax.broadcasted_iota(jnp.int32, (BLOCK, BLOCK), 1)
    row_of = lax.broadcasted_iota(jnp.int32, (BLOCK, BLOCK), 0)
    shift = jnp.where(lane == row_of, damping, 0.0)
    walkers = centred_ref.shape[0]

    def gram(index):
        return whole_ref[index * BLOCK : (index + 1) * BLOCK, :]

    def vector(first):
        halves = [whole_ref[first + j : first + j + 1, :HALF] for j in range(walkers // HALF)]
        return [jnp.concatenate(halves[j : j + 2], axis=1) for j in range(0, len(halves), 2)]

    along = vector(HALF)
    energies = vector(HALF + SUB)
    corner = whole_ref[:HALF, HALF:BLOCK].T
    lower = jnp.concatenate([corner, whole_ref[HALF:BLOCK, HALF:BLOCK]], axis=1)
    g00 = jnp.concatenate([whole_ref[:HALF, :], lower], axis=0)
    mean = sum(jnp.sum(part, axis=1, keepdims=True) for part in energies) * (1.0 / walkers)
    right = [
        (mean - energy) * (1.0 / math.sqrt(walkers)) - momentum * part
        for energy, part in zip(energies, along)
    ]
    g01, g02, g12 = gram(1), gram(2), gram(4)
    inv0 = inverse(g00 + shift)
    w01, w02 = matmul(inv0, g01), matmul(inv0, g02)
    s11 = gram(3) + shift - matmul(g01, w01, 0, 0)
    s12 = g12 - matmul(g01, w02, 0, 0)
    s22 = gram(5) + shift - matmul(g02, w02, 0, 0)
    y0 = matmul(right[0], inv0)
    r1 = right[1] - matmul(y0, g01)
    r2 = right[2] - matmul(y0, g02)
    inv1 = inverse(s11)
    w12 = matmul(inv1, s12)
    s22 = s22 - matmul(s12, w12, 0, 0)
    y1 = matmul(r1, inv1)
    r2 = r2 - matmul(y1, s12)
    w02 = w02 - matmul(w01, w12)
    column0 = row_sums(inv0, right[0]) - row_sums(w01, y1)
    column1 = row_sums(inv1, r1)
    inv2 = inverse(s22)
    x2 = matmul(r2, inv2)
    solved = (
        column0 - row_sums(w02, x2),
        column1 - row_sums(w12, x2),
        row_sums(inv2, r2),
    )
    total = jnp.zeros((SUB, out_ref.shape[1]), jnp.float32)
    for i, column in enumerate(solved):
        terms = centred_ref[i * BLOCK : (i + 1) * BLOCK, :] * column
        total = total + jnp.sum(terms.reshape(BLOCK // SUB, SUB, -1), axis=0)
    out_ref[...] = jnp.sum(total, axis=0, keepdims=True) + momentum * prev_ref[...]


def solve_update(whole, centred, prev_update):
    return pl.pallas_call(
        solve_kernel,
        in_specs=[pl.BlockSpec(memory_space=pltpu.VMEM)] * 3,
        out_specs=pl.BlockSpec(memory_space=pltpu.VMEM),
        out_shape=jax.ShapeDtypeStruct(prev_update.shape, jnp.float32),
        name="solve_update",
    )(whole, centred, prev_update)


def exchange(pieces, axes):
    return lax.all_to_all(pieces, axes, split_axis=0, concat_axis=0, tiled=True)


def hand_round(value, axes):
    return exchange(jnp.broadcast_to(value[None], (lax.axis_size(axes), *value.shape)), axes)


def body(
    jacobian,
    prev_update,
    base_energy,
    elec_pos,
    atom_pos,
    quad_ratio,
    rotation,
    channels,
    ecp_coef,
    ecp_expo,
):
    owners = lax.axis_size(WALK)
    columns = lax.axis_size(COL)
    rows, width = jacobian.shape
    walkers = rows * owners
    scale = 1.0 / (width * columns)
    pieces = dense_pieces(jacobian, owners).reshape(owners, rows * SUB, LANES)
    received = exchange(pieces, WALK)
    energy_mine = base_energy + nonlocal_energy(
        elec_pos, atom_pos, quad_ratio, rotation, channels, ecp_coef, ecp_expo
    )
    energy_row = lax.dynamic_update_slice(
        jnp.zeros((1, walkers), jnp.float32),
        energy_mine[None, :] / columns,
        (0, lax.axis_index(WALK) * rows),
    )
    packed, centred = gram_pieces(
        near(received.reshape(walkers * SUB, LANES)), prev_update, near(energy_row), walkers, scale
    )
    plane = lax.axis_size(PLANE)
    share = jnp.sum(exchange(packed.reshape(plane, -1, LANES), PLANE), axis=0)
    share = jnp.sum(hand_round(share, "z"), axis=0)
    whole = hand_round(share, PLANE)
    update_mine = solve_update(near(whole.reshape(packed.shape)), near(centred), prev_update)
    return (energy_mine, update_mine)


def solution(mesh):
    mesh = jax.sharding.Mesh(mesh.devices.reshape(16, 4, 4, 2), ("z", "y", "x", "core"))
    in_specs = (
        P(WALK, COL),
        P(COL, WALK),
        P(WALK),
        P(WALK, None, None),
        P(),
        P(WALK, None, None, None),
        P(WALK, None),
        P(),
        P(),
        P(),
    )
    out_specs = (P(WALK), P(COL, WALK))
    return jax.shard_map(body, mesh=mesh, in_specs=in_specs, out_specs=out_specs, check_vma=False)
```

```python
import math

import jax
import jax.numpy as jnp
from jax import lax
from jax.experimental import pallas as pl
from jax.experimental.pallas import tpu as pltpu
from jax.sharding import PartitionSpec as P

NROT = 16


momentum = 0.9
damping = 0.1


def icosa_points():
    golden = (1.0 + math.sqrt(5.0)) / 2.0
    length = math.sqrt(1.0 + golden * golden)
    rows = []
    for first in (-1.0, 1.0):
        for second in (-golden, golden):
            rows.append((0.0, first / length, second / length))
            rows.append((first / length, second / length, 0.0))
            rows.append((second / length, 0.0, first / length))
    return jnp.asarray(rows, dtype=jnp.float32).T


def rotation_table(count):
    angle = jnp.arange(count, dtype=jnp.float32)
    turn_z = 2.0 * math.pi * angle / count
    turn_x = 0.9 * angle
    cz, sz = (jnp.cos(turn_z), jnp.sin(turn_z))
    cx, sx = (jnp.cos(turn_x), jnp.sin(turn_x))
    zeros = jnp.zeros_like(cz)
    matrix = jnp.stack(
        [
            jnp.stack([cz, -sz * cx, sz * sx], axis=-1),
            jnp.stack([sz, cz * cx, -cz * sx], axis=-1),
            jnp.stack([zeros, sx, cx], axis=-1),
        ],
        axis=1,
    )
    points = icosa_points()
    rotated = matrix[:, :, 0, None] * points[None, 0, :]
    rotated = rotated + matrix[:, :, 1, None] * points[None, 1, :]
    rotated = rotated + matrix[:, :, 2, None] * points[None, 2, :]
    return rotated.reshape(count, -1)


def nonlocal_energy(elec_pos, atom_pos, quad_ratio, rotation, channels, ecp_coef, ecp_expo):
    walkers, electrons = rotation.shape
    count = NROT
    table = rotation_table(count)
    onehot = (rotation[:, :, None] == jnp.arange(count, dtype=jnp.int32)[None, None, :]).astype(
        jnp.float32
    )
    rotated = jnp.einsum("wek,kf->wef", onehot, table, precision=lax.Precision.HIGHEST)
    rotated = rotated.reshape(walkers, electrons, 3, -1)
    diff = elec_pos[:, :, None, :] - atom_pos[None, :, :, None]
    dist2 = jnp.sum(diff * diff, axis=1)
    unit = diff / jnp.sqrt(dist2 + 0.01)[:, None, :, :]
    cosang = unit[:, 0, :, :, None] * rotated[:, None, :, 0, :]
    cosang = cosang + unit[:, 1, :, :, None] * rotated[:, None, :, 1, :]
    cosang = cosang + unit[:, 2, :, :, None] * rotated[:, None, :, 2, :]
    quad = quad_ratio.shape[-1]
    lmax = ecp_coef.shape[1]
    lower = jnp.ones_like(cosang)
    upper = cosang
    total = jnp.zeros((walkers,), jnp.float32)
    for level in range(lmax):
        if level == 0:
            poly = lower
        elif level == 1:
            poly = upper
        else:
            fresh = ((2 * level - 1) * cosang * upper - (level - 1) * lower) / level
            lower, upper = (upper, fresh)
            poly = fresh
        angular = jnp.sum(poly * quad_ratio, axis=-1) / quad
        active = (channels > level).astype(jnp.float32)
        radial = ecp_coef[None, :, level, None] * jnp.exp(-ecp_expo[None, :, level, None] * dist2)
        term = (2 * level + 1) * active[None, :, None] * radial * angular
        total = total + jnp.sum(term, axis=(1, 2))
    return total


BLOCK = 128
HALF = 64
EXTRA = 16
PANEL = 16
SUB = 8
LANES = 128
WALK = ("z", "y")
COL = ("x", "core")
PLANE = ("core", "x", "y")


def spread_rows(jac_ref, out_ref, taken_ref, spread_ref, in_sems, out_sems):
    rows, width = jac_ref.shape
    chunks = in_sems.shape[0]
    lanes, height = width // chunks, out_ref.shape[0] // chunks
    copies_in, copies_out = [], []
    for c in range(chunks):
        part = slice(c * lanes, (c + 1) * lanes)
        copies_in.append(
            pltpu.make_async_copy(jac_ref.at[:, part], taken_ref.at[:, part], in_sems.at[c])
        )
        part = slice(c * height, (c + 1) * height)
        copies_out.append(
            pltpu.make_async_copy(spread_ref.at[part], out_ref.at[part], out_sems.at[c])
        )
    for copy in copies_in:
        copy.start()
    for c in range(chunks):
        copies_in[c].wait()
        for tile in range(c * lanes // LANES, (c + 1) * lanes // LANES):
            owner, sub = divmod(tile, SUB)
            spread_ref[pl.ds(owner * rows * SUB + sub, rows, stride=SUB), :] = taken_ref[
                :, tile * LANES : (tile + 1) * LANES
            ]
        copies_out[c].start()
    for copy in copies_out:
        copy.wait()


def dense_pieces(jacobian, owners):
    rows, width = jacobian.shape
    chunks = 8
    assert width // owners == SUB * LANES
    shape = (owners * rows * SUB, LANES)
    return pl.pallas_call(
        spread_rows,
        in_specs=[pl.BlockSpec(memory_space=pl.ANY)],
        out_specs=pl.BlockSpec(memory_space=pl.ANY),
        out_shape=jax.ShapeDtypeStruct(shape, jnp.float32),
        scratch_shapes=[
            pltpu.VMEM((rows, width), jnp.float32),
            pltpu.VMEM(shape, jnp.float32),
            pltpu.SemaphoreType.DMA((chunks,)),
            pltpu.SemaphoreType.DMA((chunks,)),
        ],
        name="dense_pieces",
    )(jacobian)


def split_high_low(value):
    high = value.astype(jnp.bfloat16)
    low = (value - high.astype(jnp.float32)).astype(jnp.bfloat16)
    return high, low


def contract_last(left, right):
    return lax.dot_general(
        left,
        right,
        (((1,), (1,)), ((), ())),
        preferred_element_type=jnp.float32,
    )


def gram_kernel(scale, x_ref, prev_ref, energy_ref, packed_ref, centred_ref):
    walkers = centred_ref.shape[0]
    blocks = walkers // BLOCK
    prev_parts = split_high_low(prev_ref[...])
    strips = [None] * blocks
    for sub in range(0, SUB, 2):
        parts = []
        for s in (sub, sub + 1):
            part = x_ref[pl.ds(s, walkers, stride=SUB), :]
            part = part - jnp.sum(part, axis=0, keepdims=True) * (1.0 / walkers)
            centred_ref[:, s * LANES : (s + 1) * LANES] = part
            parts.append(part)
        high, low = split_high_low(jnp.concatenate(parts, axis=1))
        lanes = slice(sub * LANES, (sub + 2) * LANES)
        for i in range(blocks):
            left = [part[i * BLOCK : (i + 1) * BLOCK] for part in (high, low)]
            if i == 0:
                extra = [jnp.broadcast_to(p[:, lanes], (EXTRA, 2 * LANES)) for p in prev_parts]
                left = [jnp.concatenate(pair, axis=0) for pair in zip(left, extra)]
            strip = contract_last(left[0], high[i * BLOCK :])
            strip = strip + contract_last(left[0], low[i * BLOCK :])
            strip = strip + contract_last(left[1], high[i * BLOCK :])
            strips[i] = strip if strips[i] is None else strips[i] + strip
    row = 0
    for i in range(blocks):
        strip = strips[i] * scale
        for j in range(blocks - i):
            packed_ref[row : row + BLOCK, :] = strip[:BLOCK, j * BLOCK : (j + 1) * BLOCK]
            row += BLOCK
    along = strips[0][BLOCK : BLOCK + 1, :] * scale
    for j in range(walkers // HALF):
        part = slice(j * HALF, (j + 1) * HALF)
        packed_ref[HALF + j : HALF + j + 1, :HALF] = along[:, part]
        packed_ref[HALF + SUB + j : HALF + SUB + j + 1, :HALF] = energy_ref[:, part]


def gram_pieces(received, prev_update, energy_row, walkers, scale):
    width = prev_update.shape[1]
    blocks = walkers // BLOCK
    pieces = blocks * (blocks + 1) // 2
    return pl.pallas_call(
        lambda *refs: gram_kernel(scale, *refs),
        in_specs=[pl.BlockSpec(memory_space=pltpu.VMEM)] * 3,
        out_specs=[pl.BlockSpec(memory_space=pltpu.VMEM)] * 2,
        out_shape=(
            pltpu.VMEM((pieces * BLOCK, LANES), jnp.float32),
            pltpu.VMEM((walkers, width), jnp.float32),
        ),
        name="gram_pieces",
    )(received, prev_update, energy_row)


def near(value):
    return pltpu.with_memory_space_constraint(value, pltpu.VMEM)


def split_three(value):
    high, low = split_high_low(value)
    rest = value - high.astype(jnp.float32)
    return high, low, (rest - low.astype(jnp.float32)).astype(jnp.bfloat16)


def matmul(left, right, left_dim=1, right_dim=0):
    lh, lm, ll = split_three(left)
    rh, rm, rl = split_three(right)
    return lax.dot_general(
        jnp.concatenate([lh, lh, lm, lm, lh, ll], axis=left_dim),
        jnp.concatenate([rh, rm, rh, rm, rl, rh], axis=right_dim),
        (((left_dim,), (right_dim,)), ((), ())),
        preferred_element_type=jnp.float32,
    )


def reduce_panel(panel, first):
    full = (PANEL, BLOCK)
    lane = lax.broadcasted_iota(jnp.int32, full, 1)
    row_of = lax.broadcasted_iota(jnp.int32, full, 0)
    pivots = [jnp.broadcast_to(panel[:, first + k : first + k + 1], full) for k in range(PANEL)]
    for k in range(PANEL):
        column = pivots[k]
        scale = 1.0 / jnp.broadcast_to(column[k : k + 1, :], full)
        mine = row_of == k
        here = lane == first + k
        row = jnp.broadcast_to(panel[k : k + 1, :], full)
        row = jnp.where(here, scale, row * scale)
        panel = jnp.where(mine, row, jnp.where(here, 0.0, panel) - column * row)
        for j in range(k + 1, PANEL):
            other = jnp.broadcast_to(pivots[j][k : k + 1, :], full) * scale
            pivots[j] = jnp.where(mine, other, pivots[j] - column * other)
    return panel


def inverse(block):
    full = (PANEL, BLOCK)
    lane = lax.broadcasted_iota(jnp.int32, full, 1)
    groups = [block[i : i + PANEL] for i in range(0, BLOCK, PANEL)]
    for g, first in enumerate(range(0, BLOCK, PANEL)):
        panel = reduce_panel(groups[g], first)
        rows = [jnp.broadcast_to(panel[k : k + 1, :], full) for k in range(PANEL)]
        here = (lane >= first) & (lane < first + PANEL)
        for i in [*range(g + 1, len(groups)), *range(g)]:
            left = jnp.where(here, 0.0, groups[i])
            for k in range(PANEL):
                left = left - groups[i][:, first + k : first + k + 1] * rows[k]
            groups[i] = left
        groups[g] = panel
    return jnp.concatenate(groups, axis=0)


def solve_kernel(whole_ref, centred_ref, prev_ref, out_ref):
    lane = lax.broadcasted_iota(jnp.int32, (BLOCK, BLOCK), 1)
    row_of = lax.broadcasted_iota(jnp.int32, (BLOCK, BLOCK), 0)
    shift = jnp.where(lane == row_of, damping, 0.0)
    walkers = centred_ref.shape[0]

    def gram(index):
        return whole_ref[index * BLOCK : (index + 1) * BLOCK, :]

    def vector(first):
        halves = [whole_ref[first + j : first + j + 1, :HALF] for j in range(walkers // HALF)]
        return [jnp.concatenate(halves[j : j + 2], axis=1) for j in range(0, len(halves), 2)]

    along = vector(HALF)
    energies = vector(HALF + SUB)
    corner = whole_ref[:HALF, HALF:BLOCK].T
    lower = jnp.concatenate([corner, whole_ref[HALF:BLOCK, HALF:BLOCK]], axis=1)
    g00 = jnp.concatenate([whole_ref[:HALF, :], lower], axis=0)
    mean = sum(jnp.sum(part, axis=1, keepdims=True) for part in energies) * (1.0 / walkers)
    right = [
        (mean - energy) * (1.0 / math.sqrt(walkers)) - momentum * part
        for energy, part in zip(energies, along)
    ]
    g01, g02, g12 = gram(1), gram(2), gram(4)
    inv0 = inverse(g00 + shift)
    w01, w02 = matmul(inv0, g01), matmul(inv0, g02)
    s11 = gram(3) + shift - matmul(g01, w01, 0, 0)
    s12 = g12 - matmul(g01, w02, 0, 0)
    s22 = gram(5) + shift - matmul(g02, w02, 0, 0)
    y0 = matmul(right[0], inv0)
    r1 = right[1] - matmul(y0, g01)
    r2 = right[2] - matmul(y0, g02)
    inv1 = inverse(s11)
    w12 = matmul(inv1, s12)
    s22 = s22 - matmul(s12, w12, 0, 0)
    y1 = matmul(r1, inv1)
    r2 = r2 - matmul(y1, s12)
    y0 = y0 - matmul(y1, w01, 1, 1)
    w02 = w02 - matmul(w01, w12)
    inv2 = inverse(s22)
    x2 = matmul(r2, inv2)
    x1 = y1 - matmul(x2, w12, 1, 1)
    x0 = y0 - matmul(x2, w02, 1, 1)
    total = jnp.zeros((SUB, out_ref.shape[1]), jnp.float32)
    for i, solved in enumerate((x0, x1, x2)):
        solved = jnp.broadcast_to(solved, (BLOCK, BLOCK))
        column = jnp.sum(jnp.where(lane == row_of, solved, 0.0), axis=1, keepdims=True)
        terms = centred_ref[i * BLOCK : (i + 1) * BLOCK, :] * column
        total = total + jnp.sum(terms.reshape(BLOCK // SUB, SUB, -1), axis=0)
    out_ref[...] = jnp.sum(total, axis=0, keepdims=True) + momentum * prev_ref[...]


def solve_update(whole, centred, prev_update):
    return pl.pallas_call(
        solve_kernel,
        in_specs=[pl.BlockSpec(memory_space=pltpu.VMEM)] * 3,
        out_specs=pl.BlockSpec(memory_space=pltpu.VMEM),
        out_shape=jax.ShapeDtypeStruct(prev_update.shape, jnp.float32),
        name="solve_update",
    )(whole, centred, prev_update)


def exchange(pieces, axes):
    return lax.all_to_all(pieces, axes, split_axis=0, concat_axis=0, tiled=True)


def hand_round(value, axes):
    return exchange(jnp.broadcast_to(value[None], (lax.axis_size(axes), *value.shape)), axes)


def body(
    jacobian,
    prev_update,
    base_energy,
    elec_pos,
    atom_pos,
    quad_ratio,
    rotation,
    channels,
    ecp_coef,
    ecp_expo,
):
    owners = lax.axis_size(WALK)
    columns = lax.axis_size(COL)
    rows, width = jacobian.shape
    walkers = rows * owners
    scale = 1.0 / (width * columns)
    pieces = dense_pieces(jacobian, owners).reshape(owners, rows * SUB, LANES)
    received = exchange(pieces, WALK)
    energy_mine = base_energy + nonlocal_energy(
        elec_pos, atom_pos, quad_ratio, rotation, channels, ecp_coef, ecp_expo
    )
    energy_row = lax.dynamic_update_slice(
        jnp.zeros((1, walkers), jnp.float32),
        energy_mine[None, :] / columns,
        (0, lax.axis_index(WALK) * rows),
    )
    packed, centred = gram_pieces(
        near(received.reshape(walkers * SUB, LANES)), prev_update, near(energy_row), walkers, scale
    )
    plane = lax.axis_size(PLANE)
    share = jnp.sum(exchange(packed.reshape(plane, -1, LANES), PLANE), axis=0)
    share = jnp.sum(hand_round(share, "z"), axis=0)
    whole = hand_round(share, PLANE)
    update_mine = solve_update(near(whole.reshape(packed.shape)), near(centred), prev_update)
    return (energy_mine, update_mine)


def solution(mesh):
    mesh = jax.sharding.Mesh(mesh.devices.reshape(16, 4, 4, 2), ("z", "y", "x", "core"))
    in_specs = (
        P(WALK, COL),
        P(COL, WALK),
        P(WALK),
        P(WALK, None, None),
        P(),
        P(WALK, None, None, None),
        P(WALK, None),
        P(),
        P(),
        P(),
    )
    out_specs = (P(WALK), P(COL, WALK))
    return jax.shard_map(body, mesh=mesh, in_specs=in_specs, out_specs=out_specs, check_vma=False)
```
